32 devices in a mesh: gx: 4 (over y, core), gy: 8 (over z, x).
Axes of the slice: x: 2, y: 2, z: 4, core: 2. Of those that a mesh axis runs over, the one named last changes fastest.
Arguments:
- permeability: float32 [3, 8, 32, 1024], P(None, None, 'gx', 'gy'), may hold values from 0.01 to 10
- layer_map: int32 [8], replicated, may hold values from 0 to 3, never falling along the last dimension, each value on 1 to 3 neighbouring positions
Outputs:
- coarse_perm: float32 [3, 4, 4, 128], P(None, None, 'gx', 'gy')
- coarse_trans: float32 [3, 4, 4, 128], P(None, None, 'gx', 'gy')
The draws below stay inside these ranges and needn't reach their ends.
Inputs may be any that keep to these rules, and one draw needn't show every extreme that they name: layer_map never falls along the fine layers and every one of the 4 coarse layers holds one or more fine layers.
All inputs are finite; a program needn't handle non-finite values.
Results may differ from the reference program's by a relative error of at most 0.0003.
Values sent between devices are 32-bit elements; how exact they have to be, the bound alone decides.
No kernel may reach another device: no remote copies, remote signals or barrier semaphores. Data moves between devices by JAX's collectives and lax.ppermute only.
A program may use at most 64 MiB of HBM per device.

```python
import math
import jax
import jax.numpy as jnp
import numpy as np
from jax import lax

NZ = 8
NCL = 4
BXY = 8
SWEEPS = 4
NX = 32
NY = 1024
N_GX = 4
N_GY = 8


def steps_of(key, shape, shards, least, high):
    gain = 1.0
    for axis_at, parts in shards:
        steps = jax.random.uniform(jax.random.fold_in(jax.random.fold_in(key, 6), axis_at), (parts,), jnp.float32, least / len(shards), high / len(shards))
        gain = gain * jnp.repeat(jnp.exp(steps), shape[axis_at] // parts).reshape((-1,) + (1,) * (len(shape) - 1 - axis_at))
    return gain


def profile(number_of, total, most, lean):
    loads = [(1 << 20) // math.isqrt(rank ** lean) + 1 for rank in range(2, number_of + 1)]
    spare, given = total - most - (number_of - 1), [1] * (number_of - 1)
    while spare > 0:
        candidates = [i for i in range(number_of - 1) if given[i] < most]
        whole, budget = sum([loads[i] for i in candidates]), spare
        for i in candidates:
            more = min(most - given[i], max(1, budget * loads[i] // whole), spare)
            given[i] = given[i] + more
            spare = spare - more
    return np.array([most] + given)


def ragged_sizes(rng, number_of, total, reach, skew):
    if number_of == 2:
        one = jax.random.randint(rng, (), max(1, total - reach), min(reach, total - 1) + 1)
        return jnp.stack([one, total - one])
    tallies = jnp.asarray(profile(number_of, total, reach, skew), jnp.int32)
    pairs = (number_of - 1) // 2
    giver, receiver = tallies[1:1 + 2 * pairs:2], tallies[2:2 + 2 * pairs:2]
    room = jnp.minimum(giver - 1, reach - receiver)
    passed = jax.random.randint(jax.random.fold_in(rng, 1), (pairs,), 0, 1 << 20) % (room + 1)
    tallies = tallies.at[1:1 + 2 * pairs:2].set(giver - passed).at[2:2 + 2 * pairs:2].set(receiver + passed)
    return tallies[jax.random.permutation(jax.random.fold_in(rng, 2), number_of)]


def setup_inputs(seed: int = 0) -> dict:
    seeds = jax.random.split(jax.random.key(seed), 3)
    permeability = jnp.clip(jnp.exp(math.log(10.0) - 6.9077553 * jax.random.uniform(seeds[0], (3, NZ, NX, NY), jnp.float32) ** steps_of(seeds[0], (3, NZ, NX, NY), ((2, 4), (3, 8)), -0.2, 0.2)), 0.01, 10.0)
    layer_map = jnp.searchsorted(jnp.cumsum(ragged_sizes(seeds[1], NCL, NZ, NZ // NCL + NZ // (2 * NCL), 0)), jnp.arange(NZ), side="right").astype(jnp.int32)
    return dict(permeability=permeability, layer_map=layer_map)


KMIN = 0.01
EPS = 1e-6


def sweep_weights(count):
    return [1.0 / (1.05 + 0.95 * math.cos(math.pi * (2 * s + 1) / (2 * count))) for s in range(count)]


def harmonic(left, right):
    return 2.0 * left * right / (left + right)


def linear_field(depth, width, height):
    zc = (jnp.arange(depth + 2, dtype=jnp.float32) - 0.5 - depth / 2.0) / depth
    xc = (jnp.arange(width + 2, dtype=jnp.float32) - 0.5 - width / 2.0) / width
    yc = (jnp.arange(height + 2, dtype=jnp.float32) - 0.5 - height / 2.0) / height
    shape = (depth + 2, width + 2, height + 2)
    return jnp.stack([jnp.broadcast_to(xc[None, :, None], shape), jnp.broadcast_to(yc[None, None, :], shape), jnp.broadcast_to(zc[:, None, None], shape)])


def patch_partials(kext, layer_map):
    depth, width, height = kext.shape[1], kext.shape[2], kext.shape[3]
    perm = kext + KMIN
    tx = jnp.concatenate([perm[0][:, :1], harmonic(perm[0][:, :-1], perm[0][:, 1:]), perm[0][:, -1:]], axis=1)
    ty = jnp.concatenate([perm[1][:, :, :1], harmonic(perm[1][:, :, :-1], perm[1][:, :, 1:]), perm[1][:, :, -1:]], axis=2)
    tz = jnp.concatenate([perm[2][:1], harmonic(perm[2][:-1], perm[2][1:]), perm[2][-1:]], axis=0)
    diag = tx[:, :-1] + tx[:, 1:] + ty[:, :, :-1] + ty[:, :, 1:] + tz[:-1] + tz[1:]
    inverse = 1.0 / diag
    ghost = linear_field(depth, width, height)

    def residual(pressure):
        full = ghost.at[:, 1:-1, 1:-1, 1:-1].set(pressure)
        inflow = tx[:, 1:] * full[:, 1:-1, 2:, 1:-1] + tx[:, :-1] * full[:, 1:-1, :-2, 1:-1]
        inflow = inflow + ty[:, :, 1:] * full[:, 1:-1, 1:-1, 2:] + ty[:, :, :-1] * full[:, 1:-1, 1:-1, :-2]
        inflow = inflow + tz[1:] * full[:, 2:, 1:-1, 1:-1] + tz[:-1] * full[:, :-2, 1:-1, 1:-1]
        return inflow - diag * pressure

    pressure = ghost[:, 1:-1, 1:-1, 1:-1]
    for weight in sweep_weights(SWEEPS):
        pressure = pressure + weight * (residual(pressure) * inverse)
    full = ghost.at[:, 1:-1, 1:-1, 1:-1].set(pressure)
    drop = jnp.stack([full[0, 1:-1, 1:-1, 1:-1] - full[0, 1:-1, 2:, 1:-1], full[1, 1:-1, 1:-1, 1:-1] - full[1, 1:-1, 1:-1, 2:], full[2, 1:-1, 1:-1, 1:-1] - full[2, 2:, 1:-1, 1:-1]])
    faces = jnp.stack([tx[:, 1:], ty[:, :, 1:], tz[1:]])
    square = drop * drop
    energy = faces * square
    onehot = (layer_map[:, None] == jnp.arange(NCL, dtype=jnp.int32)[None, :]).astype(jnp.float32)

    def coarsen(values):
        blocks = values.reshape(3, depth, width // BXY, BXY, height // BXY, BXY).sum(axis=(3, 5))
        return jnp.einsum("dzab,zl->dlab", blocks, onehot, precision=lax.Precision.HIGHEST)

    return coarsen(energy), coarsen(square)


def reference(permeability, layer_map):
    cols_x = permeability.shape[2] // N_GX
    cols_y = permeability.shape[3] // N_GY
    padded = jnp.pad(permeability, ((0, 0), (0, 0), (BXY, BXY), (BXY, BXY)))
    blocks_x = cols_x // BXY
    blocks_y = cols_y // BXY

    def one_row(row):
        def one_patch(col):
            start = (jnp.int32(0), jnp.int32(0), (row * cols_x).astype(jnp.int32), (col * cols_y).astype(jnp.int32))
            kext = lax.dynamic_slice(padded, start, (3, NZ, cols_x + 2 * BXY, cols_y + 2 * BXY))
            return patch_partials(kext, layer_map)
        return jax.vmap(one_patch)(jnp.arange(N_GY, dtype=jnp.int32))

    energy, square = lax.map(one_row, jnp.arange(N_GX, dtype=jnp.int32))
    shape = (3, NCL, N_GX * blocks_x + 2, N_GY * blocks_y + 2)
    size = (3, NCL, blocks_x + 2, blocks_y + 2)

    def accumulate(index, totals):
        row = (index // N_GY).astype(jnp.int32)
        col = (index % N_GY).astype(jnp.int32)
        start = (jnp.int32(0), jnp.int32(0), (row * blocks_x).astype(jnp.int32), (col * blocks_y).astype(jnp.int32))
        total_e, total_s = totals
        total_e = lax.dynamic_update_slice(total_e, lax.dynamic_slice(total_e, start, size) + energy[row, col], start)
        total_s = lax.dynamic_update_slice(total_s, lax.dynamic_slice(total_s, start, size) + square[row, col], start)
        return total_e, total_s

    zeros = jnp.zeros(shape, jnp.float32)
    total_e, total_s = lax.fori_loop(0, N_GX * N_GY, accumulate, (zeros, zeros))
    coarse_perm = total_e[:, :, 1:-1, 1:-1] / (total_s[:, :, 1:-1, 1:-1] + EPS)
    nxt_x = jnp.concatenate([coarse_perm[0][:, 1:], jnp.zeros_like(coarse_perm[0][:, :1])], axis=1)
    nxt_y = jnp.concatenate([coarse_perm[1][:, :, 1:], jnp.zeros_like(coarse_perm[1][:, :, :1])], axis=2)
    trans_x = harmonic(coarse_perm[0], nxt_x)
    trans_y = harmonic(coarse_perm[1], nxt_y)
    trans_z = jnp.concatenate([harmonic(coarse_perm[2][:-1], coarse_perm[2][1:]), jnp.zeros_like(coarse_perm[2][:1])], axis=0)
    return coarse_perm, jnp.stack([trans_x, trans_y, trans_z])
```

```python
import functools
import math

import jax
import jax.numpy as jnp
from jax import lax
from jax.experimental import pallas as pl
from jax.experimental.pallas import tpu as pltpu
from jax.sharding import PartitionSpec as P

NCL = 4
BXY = 8
SWEEPS = 4
KMIN = 0.01
EPS = 1e-06

LOW = SWEEPS
HIGH = SWEEPS + 1
RIGHT = BXY + HIGH
SLOT = LOW + RIGHT
FIRST, LAST = -LOW, 2 * BXY + HIGH - 1


def sweep_weights(count):
    return [
        1.0 / (1.05 + 0.95 * math.cos(math.pi * (2 * s + 1) / (2 * count))) for s in range(count)
    ]


WEIGHTS = sweep_weights(SWEEPS)


def harmonic(left, right):
    return 2.0 * left * right / (left + right)


def lanes_of(shape):
    return lax.broadcasted_iota(jnp.int32, shape, len(shape) - 1)


def up(value, axis):
    return pltpu.roll(value, value.shape[axis] - 1, axis)


def down(value, axis):
    return pltpu.roll(value, 1, axis)


def raw_row(tiles, comp, row):
    own, low, high, high2 = tiles
    ref, at = (
        (low, row + BXY)
        if row < 0
        else (own, row)
        if row < BXY
        else (high, row - BXY)
        if row < 2 * BXY
        else (high2, row - 2 * BXY)
    )
    return ref[comp, :, at, :]


def exists(row, present):
    low, high, high2 = present
    return low if row < 0 else None if row < BXY else high if row < 2 * BXY else high2


class Solver:
    def __init__(self, perm, scratch, y_ends, y_starts):
        self.perm_of = perm
        self.scratch = scratch
        self.slots = {}
        self.cache = {}
        shape = scratch.shape[1:]
        layer = lax.broadcasted_iota(jnp.int32, shape, 0)
        self.top = layer == shape[0] - 1
        self.bottom = layer == 0
        self.y_ends = y_ends
        self.y_starts = y_starts

    def memo(self, key, make):
        if key not in self.cache:
            self.cache[key] = make()
        return self.cache[key]

    def stored(self, key, make):
        if key not in self.slots:
            values = make()
            base = sum(n for _, n in self.slots.values())
            self.slots[key] = (base, len(values))
            for i, value in enumerate(values):
                self.scratch[base + i] = value
        base, _ = self.slots[key]
        return lambda i: self.scratch[base + i]

    def perm(self, comp, row):
        return self.memo(("k", comp, row), lambda: self.perm_of(comp, row))

    def tx(self, row):
        return self.memo(("tx", row), lambda: harmonic(self.perm(0, row), self.perm(0, row + 1)))

    def tyz(self, row):
        def make():
            ky, kz = self.perm(1, row), self.perm(2, row)
            ty = harmonic(ky, up(ky, 1))
            if self.y_ends is not None:
                ty = jnp.where(self.y_ends, ky, ty)
            ty_low = down(ty, 1)
            if self.y_starts is not None:
                ty_low = jnp.where(self.y_starts, ky, ty_low)
            tz = jnp.where(self.top, kz, harmonic(kz, up(kz, 0)))
            tz_low = jnp.where(self.bottom, kz, down(tz, 0))
            return ty, ty_low, tz, tz_low

        return self.memo(("tyz", row), make)

    def faces(self, row, edge):
        upper = self.perm(0, row) if edge == "up" else self.tx(row)
        lower = self.perm(0, row) if edge == "low" else self.tx(row - 1)
        return upper, lower

    def edge_of(self, row, boundary):
        return boundary[0] if boundary is not None and boundary[1] == row else None

    def coefficients(self, row, boundary):
        edge = self.edge_of(row, boundary)

        def make():
            upper, lower = self.faces(row, edge)
            ty, ty_low, tz, tz_low = self.tyz(row)
            inverse = 1.0 / (((upper + lower) + (ty + ty_low)) + (tz + tz_low))
            zero = jnp.zeros_like(inverse)
            ax = zero if edge == "up" else upper * inverse
            ax_low = zero if edge == "low" else lower * inverse
            ay, ay_low = ty * inverse, ty_low * inverse
            az, az_low = tz * inverse, tz_low * inverse
            drive = ((upper - lower) * inverse, ay - ay_low, az - az_low)
            if self.y_ends is not None:
                ay = jnp.where(self.y_ends, 0.0, ay)
            if self.y_starts is not None:
                ay_low = jnp.where(self.y_starts, 0.0, ay_low)
            az = jnp.where(self.top, 0.0, az)
            az_low = jnp.where(self.bottom, 0.0, az_low)
            return (ax, ax_low, ay, ay_low, az, az_low) + drive

        return self.stored(("c", row, edge), make)

    def pressure(self, d, count, row, boundary):
        if boundary is not None:
            kind, at = boundary
            if abs(row - at) >= count:
                boundary = None

        def make():
            c = self.coefficients(row, boundary)
            edge = self.edge_of(row, boundary)
            if count == 1:
                return WEIGHTS[0] * c(6 + d)
            here = self.pressure(d, count - 1, row, boundary)
            total = c(6 + d)
            if edge != "up":
                total = total + c(0) * self.pressure(d, count - 1, row + 1, boundary)
            if edge != "low":
                total = total + c(1) * self.pressure(d, count - 1, row - 1, boundary)
            side = c(2) * up(here, 1) + c(3) * down(here, 1)
            total = total + side
            total = total + (c(4) * up(here, 0) + c(5) * down(here, 0))
            return here + WEIGHTS[count - 1] * (total - here)

        return self.memo(("u", d, count, row, boundary), make)

    def sums(self, d, row, boundary):
        if boundary is not None:
            kind, at = boundary
            reach = SWEEPS + (1 if d == 0 and kind == "up" else 0)
            if abs(row - at) >= reach:
                boundary = None

        def make():
            here = self.pressure(d, SWEEPS, row, boundary)
            edge = self.edge_of(row, boundary)
            if d == 0:
                face = self.faces(row, edge)[0]
                above = None if edge == "up" else self.pressure(d, SWEEPS, row + 1, boundary)
            elif d == 1:
                face = self.tyz(row)[0]
                above = up(here, 1)
                if self.y_ends is not None:
                    above = jnp.where(self.y_ends, 0.0, above)
            else:
                face = self.tyz(row)[2]
                above = jnp.where(self.top, 0.0, up(here, 0))
            drop = (1.0 - here) if above is None else (1.0 - here) + above
            square = drop * drop
            return face * square, square

        return self.memo(("s", d, row, boundary), make)

    def block(self, d, begin, patches):
        groups = {}
        for row in range(begin, begin + BXY):
            for boundary, weight in patches:
                pair = self.sums(d, row, boundary)
                groups.setdefault(id(weight), (weight, []))[1].append(pair)
        totals = None
        for weight, pairs in groups.values():
            part = [functools.reduce(jnp.add, parts) for parts in zip(*pairs)]
            if weight is not None:
                part = [weight * p for p in part]
            totals = part if totals is None else [a + b for a, b in zip(totals, part)]
        return totals


def accumulate(solver, present):
    low, high, high2 = present
    own = [(("up", BXY - 1), low), (None, None), (("low", 0), high)]
    after = [(("up", 2 * BXY - 1), None), (None, None), (("low", BXY), high2)]
    jobs = [(d, 0, own) for d in range(3)] + [(0, BXY, after)]
    results = {}
    order = [jobs[0], jobs[1], jobs[2], jobs[3]]
    for row in range(BXY):
        for d, begin, patches in order:
            for boundary, _ in patches:
                solver.sums(d, begin + row, boundary)
    for i, (d, begin, patches) in enumerate(jobs):
        results[i] = solver.block(d, begin, patches)
    return [value for i in range(len(jobs)) for value in results[i]]


def reduce_sums(sums, layer_map, columns):
    depth = sums[0].shape[0]
    stacked = jnp.concatenate(sums, axis=0)
    by_column = jnp.dot(
        stacked, columns, precision=lax.Precision.HIGHEST, preferred_element_type=jnp.float32
    )
    rows, cols = len(sums) * NCL, len(sums) * depth
    r = lax.broadcasted_iota(jnp.int32, (rows, cols), 0)
    c = lax.broadcasted_iota(jnp.int32, (rows, cols), 1)
    layer = jnp.zeros((rows, cols), jnp.int32)
    for z in range(depth):
        layer = jnp.where(c % depth == z, layer_map[z], layer)
    picks = ((r // NCL == c // depth) & (r % NCL == layer)).astype(jnp.float32)
    return jnp.dot(
        picks, by_column, precision=lax.Precision.HIGHEST, preferred_element_type=jnp.float32
    )


def flags(x_axis, y_axis):
    i, j = lax.axis_index(x_axis), lax.axis_index(y_axis)
    nx, ny = lax.axis_size(x_axis), lax.axis_size(y_axis)
    one = lambda test: jnp.where(test, 1.0, 0.0).astype(jnp.float32)
    return i, j, (one(i > 0), one(i < nx - 1), one(i < nx - 2)), (one(j > 0), one(j < ny - 1))


def packed_rows():
    return [(comp, row) for row in range(FIRST, LAST + 1) for comp in range(3)]


def pack_kernel(own, low, high, high2, out):
    lanes = own.shape[3]
    per = lanes // SLOT
    lane = lanes_of((own.shape[1], lanes))
    rows = packed_rows()
    for first in range(0, len(rows), per):
        packed = None
        for slot, (comp, row) in enumerate(rows[first : first + per]):
            value = raw_row((own, low, high, high2), comp, row)
            value = pltpu.roll(value, (LOW + SLOT * slot) % lanes, 1)
            packed = value if packed is None else jnp.where(lane < SLOT * slot, packed, value)
        out[first // per] = packed


def main_kernel(layer_map, own, low, high, high2, out, scratch):
    _, _, present, _ = flags("gx", "gy")
    tiles = (own, low, high, high2)

    def perm(comp, row):
        value = raw_row(tiles, comp, row)
        there = exists(row, present)
        return (value if there is None else value * there) + KMIN

    solver = Solver(perm, scratch, None, None)
    sums = accumulate(solver, present)
    lanes = own.shape[3]
    r = lax.broadcasted_iota(jnp.int32, (lanes, lanes), 0)
    c = lax.broadcasted_iota(jnp.int32, (lanes, lanes), 1)
    inner = (r // BXY == c) & (c > 0) & (c < lanes // BXY - 1)
    out[...] = reduce_sums(sums, layer_map, inner.astype(jnp.float32))


def edge_kernel(layer_map, own, low, high, high2, even, odd, inner, perm_out, trans_out, scratch):
    i, j, present, (has_left, has_right) = flags("gx", "gy")
    tiles = (own, low, high, high2)
    depth, lanes = own.shape[1], own.shape[3]
    per = lanes // SLOT
    lane = lanes_of((depth, lanes))
    half = lanes // 2
    last = lanes - BXY - LOW
    left = RIGHT + 7
    start = left + LOW
    stop = start + BXY + HIGH
    in_left = lane % SLOT < LOW
    is_odd = j % 2 == 1
    from_even = in_left == (jnp.zeros_like(lane) + is_odd.astype(jnp.int32) == 1)
    keep = jnp.where(in_left, has_left, has_right)
    packs = {}

    def pack(at):
        if at not in packs:
            packs[at] = jnp.where(from_even, even[at], odd[at]) * keep
        return packs[at]

    index = {key: at for at, key in enumerate(packed_rows())}
    second = (lane >= half - BXY - LOW) & (lane < half + stop)

    def perm(comp, row):
        at = index[comp, row]
        slot = at % per
        mine = raw_row(tiles, comp, row)
        theirs = pack(at // per)
        right = pltpu.roll(theirs, (-(SLOT * slot + LOW)) % lanes, 1)
        before = pltpu.roll(theirs, (left - SLOT * slot) % lanes, 1)
        value = jnp.where(lane < RIGHT, right, mine)
        value = jnp.where((lane >= left) & (lane < stop), pltpu.roll(mine, start, 1), value)
        value = jnp.where((lane >= left) & (lane < start), before, value)
        value = jnp.where(second, pltpu.roll(value, half, 1), value)
        there = exists(row, present)
        return (value if there is None else value * there) + KMIN

    y_ends = (lane == BXY - 1) | (lane == half + start + BXY - 1)
    y_starts = lane == half - BXY
    solver = Solver(perm, scratch, y_ends, y_starts)
    sums = accumulate(solver, present)
    r = lax.broadcasted_iota(jnp.int32, (lanes, lanes), 0)
    c = lax.broadcasted_iota(jnp.int32, (lanes, lanes), 1)
    count = lanes // BXY

    def span(begin):
        return (r >= begin) & (r < begin + BXY)

    first = jnp.where(span(start), 1.0, 0.0) + jnp.where(span(half + start), has_left, 0.0)
    final = jnp.where(span(lanes - BXY), 1.0, 0.0) + jnp.where(span(half - BXY), has_right, 0.0)
    beyond = jnp.where(span(0) | span(half), has_right, 0.0)
    columns = jnp.where(
        c == 0, first, jnp.where(c == count - 1, final, jnp.where(c == count, beyond, 0.0))
    )
    total = inner[...] + reduce_sums(sums, layer_map, columns)
    cells = (own.shape[2] + 2 * BXY, lanes + 2 * BXY, depth)
    energy = [total[2 * NCL * q : 2 * NCL * q + NCL] for q in range(4)]
    square = [total[2 * NCL * q + NCL : 2 * NCL * (q + 1)] for q in range(4)]
    perms = [
        energy[q] / (square[q] + EPS * float(cells[d]) ** 2) for q, d in enumerate((0, 1, 2, 0))
    ]
    layer = lax.broadcasted_iota(jnp.int32, perms[0].shape, 0)
    trans = [
        harmonic(perms[0], perms[3] * present[1]),
        harmonic(perms[1], up(perms[1], 1)),
    ]
    above = jnp.concatenate([perms[2][1:], jnp.zeros_like(perms[2][:1])], axis=0)
    trans.append(harmonic(perms[2], above))
    for d in range(3):
        for l in range(NCL):
            perm_out[d, l, :, :] = perms[d][l : l + 1, :count]
            trans_out[d, l, :, :] = trans[d][l : l + 1, :count]


def ring(value, axis, steps):
    count = lax.axis_size(axis)
    return lax.ppermute(value, axis, [(s, (s + steps) % count) for s in range(count)])


def swap(value, axes, parity):
    nx, ny = (lax.axis_size(a) for a in axes)
    pairs = []
    for i in range(nx):
        for j in range(ny):
            other = j ^ 1 if parity == 0 else ((j - 1) ^ 1) + 1
            if 0 <= other < ny:
                pairs.append((i * ny + j, i * ny + other))
            else:
                pairs.append((i * ny + j, (i ^ 1 if nx % 2 == 0 else i) * ny + j))
    return lax.ppermute(value, axes, pairs)


def local(permeability, layer_map):
    _, depth, width, lanes = permeability.shape
    if width != BXY or depth != 8 or lanes != 128:
        raise ValueError("unsupported tile")
    tiles = (
        permeability,
        ring(permeability, "gx", 1),
        ring(permeability, "gx", -1),
        ring(permeability, "gx", -2),
    )
    vmem = pl.BlockSpec(memory_space=pltpu.VMEM)
    smem = pl.BlockSpec(memory_space=pltpu.SMEM)
    count = len(packed_rows())
    per = lanes // SLOT
    packed = pl.pallas_call(
        pack_kernel,
        out_shape=jax.ShapeDtypeStruct((-(-count // per), depth, lanes), jnp.float32),
        in_specs=[vmem] * 4,
        out_specs=vmem,
    )(*tiles)
    even = swap(packed, ("gx", "gy"), 0)
    odd = swap(packed, ("gx", "gy"), 1)
    scratch = [pltpu.VMEM((256, depth, lanes), jnp.float32)]
    inner = pl.pallas_call(
        main_kernel,
        out_shape=jax.ShapeDtypeStruct((8 * NCL, lanes), jnp.float32),
        in_specs=[smem] + [vmem] * 4,
        out_specs=vmem,
        scratch_shapes=scratch,
        cost_estimate=pl.CostEstimate(flops=6_000_000, bytes_accessed=4 * permeability.size * 4, transcendentals=0),
    )(layer_map, *tiles)
    out = jax.ShapeDtypeStruct((3, NCL, width // BXY, lanes // BXY), jnp.float32)
    return pl.pallas_call(
        edge_kernel,
        out_shape=(out, out),
        in_specs=[smem] + [vmem] * 7,
        out_specs=(vmem, vmem),
        scratch_shapes=scratch,
    )(layer_map, *tiles, even, odd, inner)


def solution(mesh):
    in_specs = (P(None, None, "gx", "gy"), P())
    out_specs = (P(None, None, "gx", "gy"), P(None, None, "gx", "gy"))
    return jax.shard_map(local, mesh=mesh, in_specs=in_specs, out_specs=out_specs, check_vma=False)
```

```python
import functools
import math

import jax
import jax.numpy as jnp
from jax import lax
from jax.experimental import pallas as pl
from jax.experimental.pallas import tpu as pltpu
from jax.sharding import PartitionSpec as P

NCL = 4
BXY = 8
SWEEPS = 4
KMIN = 0.01
EPS = 1e-06

LOW = SWEEPS
HIGH = SWEEPS + 1
RIGHT = BXY + HIGH
SLOT = LOW + RIGHT
FIRST, LAST = -LOW, 2 * BXY + HIGH - 1


def sweep_weights(count):
    return [
        1.0 / (1.05 + 0.95 * math.cos(math.pi * (2 * s + 1) / (2 * count))) for s in range(count)
    ]


WEIGHTS = sweep_weights(SWEEPS)


def harmonic(left, right):
    return 2.0 * left * right / (left + right)


def lanes_of(shape):
    return lax.broadcasted_iota(jnp.int32, shape, len(shape) - 1)


def up(value, axis):
    return pltpu.roll(value, value.shape[axis] - 1, axis)


def down(value, axis):
    return pltpu.roll(value, 1, axis)


def raw_row(tiles, comp, row):
    own, low, high, high2 = tiles
    if row < 0:
        return low[row + low.shape[0], comp]
    if row < BXY:
        return own[row, comp]
    if row < 2 * BXY:
        return high[comp, :, row - BXY, :]
    return high2[row - 2 * BXY, comp]


def exists(row, present):
    low, high, high2 = present
    return low if row < 0 else None if row < BXY else high if row < 2 * BXY else high2


class Solver:
    def __init__(self, perm, scratch, y_ends, y_starts):
        self.perm_of = perm
        self.scratch = scratch
        self.slots = {}
        self.cache = {}
        shape = scratch.shape[1:]
        layer = lax.broadcasted_iota(jnp.int32, shape, 0)
        self.top = layer == shape[0] - 1
        self.bottom = layer == 0
        self.y_ends = y_ends
        self.y_starts = y_starts

    def memo(self, key, make):
        if key not in self.cache:
            self.cache[key] = make()
        return self.cache[key]

    def stored(self, key, make):
        if key not in self.slots:
            values = make()
            base = sum(n for _, n in self.slots.values())
            self.slots[key] = (base, len(values))
            for i, value in enumerate(values):
                self.scratch[base + i] = value
        base, _ = self.slots[key]
        return lambda i: self.scratch[base + i]

    def perm(self, comp, row):
        return self.memo(("k", comp, row), lambda: self.perm_of(comp, row))

    def tx(self, row):
        return self.memo(("tx", row), lambda: harmonic(self.perm(0, row), self.perm(0, row + 1)))

    def tyz(self, row):
        def make():
            ky, kz = self.perm(1, row), self.perm(2, row)
            ty = harmonic(ky, up(ky, 1))
            if self.y_ends is not None:
                ty = jnp.where(self.y_ends, ky, ty)
            ty_low = down(ty, 1)
            if self.y_starts is not None:
                ty_low = jnp.where(self.y_starts, ky, ty_low)
            tz = jnp.where(self.top, kz, harmonic(kz, up(kz, 0)))
            tz_low = jnp.where(self.bottom, kz, down(tz, 0))
            return ty, ty_low, tz, tz_low

        return self.memo(("tyz", row), make)

    def faces(self, row, edge):
        upper = self.perm(0, row) if edge == "up" else self.tx(row)
        lower = self.perm(0, row) if edge == "low" else self.tx(row - 1)
        return upper, lower

    def edge_of(self, row, boundary):
        return boundary[0] if boundary is not None and boundary[1] == row else None

    def coefficients(self, row, boundary):
        edge = self.edge_of(row, boundary)

        def make():
            upper, lower = self.faces(row, edge)
            ty, ty_low, tz, tz_low = self.tyz(row)
            inverse = 1.0 / (((upper + lower) + (ty + ty_low)) + (tz + tz_low))
            zero = jnp.zeros_like(inverse)
            ax = zero if edge == "up" else upper * inverse
            ax_low = zero if edge == "low" else lower * inverse
            ay, ay_low = ty * inverse, ty_low * inverse
            az, az_low = tz * inverse, tz_low * inverse
            drive = ((upper - lower) * inverse, ay - ay_low, az - az_low)
            if self.y_ends is not None:
                ay = jnp.where(self.y_ends, 0.0, ay)
            if self.y_starts is not None:
                ay_low = jnp.where(self.y_starts, 0.0, ay_low)
            az = jnp.where(self.top, 0.0, az)
            az_low = jnp.where(self.bottom, 0.0, az_low)
            return (ax, ax_low, ay, ay_low, az, az_low) + drive

        return self.stored(("c", row, edge), make)

    def pressure(self, d, count, row, boundary):
        if boundary is not None:
            kind, at = boundary
            if abs(row - at) >= count:
                boundary = None

        def make():
            c = self.coefficients(row, boundary)
            edge = self.edge_of(row, boundary)
            if count == 1:
                return WEIGHTS[0] * c(6 + d)
            here = self.pressure(d, count - 1, row, boundary)
            total = c(6 + d)
            if edge != "up":
                total = total + c(0) * self.pressure(d, count - 1, row + 1, boundary)
            if edge != "low":
                total = total + c(1) * self.pressure(d, count - 1, row - 1, boundary)
            side = c(2) * up(here, 1) + c(3) * down(here, 1)
            total = total + side
            total = total + (c(4) * up(here, 0) + c(5) * down(here, 0))
            return here + WEIGHTS[count - 1] * (total - here)

        return self.memo(("u", d, count, row, boundary), make)

    def sums(self, d, row, boundary):
        if boundary is not None:
            kind, at = boundary
            reach = SWEEPS + (1 if d == 0 and kind == "up" else 0)
            if abs(row - at) >= reach:
                boundary = None

        def make():
            here = self.pressure(d, SWEEPS, row, boundary)
            edge = self.edge_of(row, boundary)
            if d == 0:
                face = self.faces(row, edge)[0]
                above = None if edge == "up" else self.pressure(d, SWEEPS, row + 1, boundary)
            elif d == 1:
                face = self.tyz(row)[0]
                above = up(here, 1)
                if self.y_ends is not None:
                    above = jnp.where(self.y_ends, 0.0, above)
            else:
                face = self.tyz(row)[2]
                above = jnp.where(self.top, 0.0, up(here, 0))
            drop = (1.0 - here) if above is None else (1.0 - here) + above
            square = drop * drop
            return face * square, square

        return self.memo(("s", d, row, boundary), make)

    def block(self, d, begin, patches):
        groups = {}
        for row in range(begin, begin + BXY):
            for boundary, weight in patches:
                pair = self.sums(d, row, boundary)
                groups.setdefault(id(weight), (weight, []))[1].append(pair)
        totals = None
        for weight, pairs in groups.values():
            part = [functools.reduce(jnp.add, parts) for parts in zip(*pairs)]
            if weight is not None:
                part = [weight * p for p in part]
            totals = part if totals is None else [a + b for a, b in zip(totals, part)]
        return totals


def accumulate(solver, present):
    low, high, high2 = present
    own = [(("up", BXY - 1), low), (None, None), (("low", 0), high)]
    after = [(("up", 2 * BXY - 1), None), (None, None), (("low", BXY), high2)]
    jobs = [(d, 0, own) for d in range(3)] + [(0, BXY, after)]
    results = {}
    order = [jobs[0], jobs[1], jobs[2], jobs[3]]
    for row in range(BXY):
        for d, begin, patches in order:
            for boundary, _ in patches:
                solver.sums(d, begin + row, boundary)
    for i, (d, begin, patches) in enumerate(jobs):
        results[i] = solver.block(d, begin, patches)
    return [value for i in range(len(jobs)) for value in results[i]]


def reduce_sums(sums, layer_map, columns):
    depth = sums[0].shape[0]
    stacked = jnp.concatenate(sums, axis=0)
    by_column = jnp.dot(
        stacked, columns, precision=lax.Precision.HIGHEST, preferred_element_type=jnp.float32
    )
    rows, cols = len(sums) * NCL, len(sums) * depth
    r = lax.broadcasted_iota(jnp.int32, (rows, cols), 0)
    c = lax.broadcasted_iota(jnp.int32, (rows, cols), 1)
    layer = jnp.zeros((rows, cols), jnp.int32)
    for z in range(depth):
        layer = jnp.where(c % depth == z, layer_map[z], layer)
    picks = ((r // NCL == c // depth) & (r % NCL == layer)).astype(jnp.float32)
    return jnp.dot(
        picks, by_column, precision=lax.Precision.HIGHEST, preferred_element_type=jnp.float32
    )


def flags(x_axis, y_axis):
    i, j = lax.axis_index(x_axis), lax.axis_index(y_axis)
    nx, ny = lax.axis_size(x_axis), lax.axis_size(y_axis)
    one = lambda test: jnp.where(test, 1.0, 0.0).astype(jnp.float32)
    return i, j, (one(i > 0), one(i < nx - 1), one(i < nx - 2)), (one(j > 0), one(j < ny - 1))


def packed_rows():
    return [(comp, row) for row in range(FIRST, LAST + 1) for comp in range(3)]


def prepare_kernel(tile, own, first, last):
    for row in range(BXY):
        for comp in range(3):
            value = tile[comp, :, row, :]
            own[row, comp] = value
            if row < first.shape[0]:
                first[row, comp] = value
            if row >= BXY - last.shape[0]:
                last[row - BXY + last.shape[0], comp] = value


def pack_kernel(own, low, high, high2, out):
    depth, lanes = own.shape[2:]
    per = lanes // SLOT
    lane = lanes_of((depth, lanes))
    rows = packed_rows()
    for first in range(0, len(rows), per):
        packed = None
        for slot, (comp, row) in enumerate(rows[first : first + per]):
            value = raw_row((own, low, high, high2), comp, row)
            value = pltpu.roll(value, (LOW + SLOT * slot) % lanes, 1)
            packed = value if packed is None else jnp.where(lane < SLOT * slot, packed, value)
        out[first // per] = packed


def main_kernel(layer_map, own, low, high, high2, out, scratch):
    _, _, present, _ = flags("gx", "gy")
    tiles = (own, low, high, high2)

    def perm(comp, row):
        value = raw_row(tiles, comp, row)
        there = exists(row, present)
        return (value if there is None else value * there) + KMIN

    solver = Solver(perm, scratch, None, None)
    sums = accumulate(solver, present)
    lanes = own.shape[3]
    r = lax.broadcasted_iota(jnp.int32, (lanes, lanes), 0)
    c = lax.broadcasted_iota(jnp.int32, (lanes, lanes), 1)
    inner = (r // BXY == c) & (c > 0) & (c < lanes // BXY - 1)
    out[...] = reduce_sums(sums, layer_map, inner.astype(jnp.float32))


def edge_kernel(layer_map, own, low, high, high2, even, odd, inner, perm_out, trans_out, scratch):
    i, j, present, (has_left, has_right) = flags("gx", "gy")
    tiles = (own, low, high, high2)
    depth, lanes = own.shape[2:]
    per = lanes // SLOT
    lane = lanes_of((depth, lanes))
    half = lanes // 2
    last = lanes - BXY - LOW
    left = RIGHT + 7
    start = left + LOW
    stop = start + BXY + HIGH
    in_left = lane % SLOT < LOW
    is_odd = j % 2 == 1
    from_even = in_left == (jnp.zeros_like(lane) + is_odd.astype(jnp.int32) == 1)
    keep = jnp.where(in_left, has_left, has_right)
    packs = {}

    def pack(at):
        if at not in packs:
            packs[at] = jnp.where(from_even, even[at], odd[at]) * keep
        return packs[at]

    index = {key: at for at, key in enumerate(packed_rows())}
    second = (lane >= half - BXY - LOW) & (lane < half + stop)

    def perm(comp, row):
        at = index[comp, row]
        slot = at % per
        mine = raw_row(tiles, comp, row)
        theirs = pack(at // per)
        right = pltpu.roll(theirs, (-(SLOT * slot + LOW)) % lanes, 1)
        before = pltpu.roll(theirs, (left - SLOT * slot) % lanes, 1)
        value = jnp.where(lane < RIGHT, right, mine)
        value = jnp.where((lane >= left) & (lane < stop), pltpu.roll(mine, start, 1), value)
        value = jnp.where((lane >= left) & (lane < start), before, value)
        value = jnp.where(second, pltpu.roll(value, half, 1), value)
        there = exists(row, present)
        return (value if there is None else value * there) + KMIN

    y_ends = (lane == BXY - 1) | (lane == half + start + BXY - 1)
    y_starts = lane == half - BXY
    solver = Solver(perm, scratch, y_ends, y_starts)
    sums = accumulate(solver, present)
    r = lax.broadcasted_iota(jnp.int32, (lanes, lanes), 0)
    c = lax.broadcasted_iota(jnp.int32, (lanes, lanes), 1)
    count = lanes // BXY

    def span(begin):
        return (r >= begin) & (r < begin + BXY)

    first = jnp.where(span(start), 1.0, 0.0) + jnp.where(span(half + start), has_left, 0.0)
    final = jnp.where(span(lanes - BXY), 1.0, 0.0) + jnp.where(span(half - BXY), has_right, 0.0)
    beyond = jnp.where(span(0) | span(half), has_right, 0.0)
    columns = jnp.where(
        c == 0, first, jnp.where(c == count - 1, final, jnp.where(c == count, beyond, 0.0))
    )
    total = inner[...] + reduce_sums(sums, layer_map, columns)
    cells = (own.shape[0] + 2 * BXY, lanes + 2 * BXY, depth)
    energy = [total[2 * NCL * q : 2 * NCL * q + NCL] for q in range(4)]
    square = [total[2 * NCL * q + NCL : 2 * NCL * (q + 1)] for q in range(4)]
    perms = [
        energy[q] / (square[q] + EPS * float(cells[d]) ** 2) for q, d in enumerate((0, 1, 2, 0))
    ]
    layer = lax.broadcasted_iota(jnp.int32, perms[0].shape, 0)
    trans = [
        harmonic(perms[0], perms[3] * present[1]),
        harmonic(perms[1], up(perms[1], 1)),
    ]
    above = jnp.concatenate([perms[2][1:], jnp.zeros_like(perms[2][:1])], axis=0)
    trans.append(harmonic(perms[2], above))
    for d in range(3):
        for l in range(NCL):
            perm_out[d, l, :, :] = perms[d][l : l + 1, :count]
            trans_out[d, l, :, :] = trans[d][l : l + 1, :count]


def ring(value, axis, steps):
    count = lax.axis_size(axis)
    return lax.ppermute(value, axis, [(s, (s + steps) % count) for s in range(count)])


def swap(value, axes, parity):
    nx, ny = (lax.axis_size(a) for a in axes)
    pairs = []
    for i in range(nx):
        for j in range(ny):
            other = j ^ 1 if parity == 0 else ((j - 1) ^ 1) + 1
            if 0 <= other < ny:
                pairs.append((i * ny + j, i * ny + other))
            else:
                pairs.append((i * ny + j, (i ^ 1 if nx % 2 == 0 else i) * ny + j))
    return lax.ppermute(value, axes, pairs)


def local(permeability, layer_map):
    _, depth, width, lanes = permeability.shape
    if width != BXY or depth != 8 or lanes != 128:
        raise ValueError("unsupported tile")
    vmem = pl.BlockSpec(memory_space=pltpu.VMEM)
    smem = pl.BlockSpec(memory_space=pltpu.SMEM)
    count = len(packed_rows())
    per = lanes // SLOT
    limit = pltpu.CompilerParams(vmem_limit_bytes=16 << 20)
    high = ring(permeability, "gx", -1)
    rows = [pltpu.VMEM((n, 3, depth, lanes), jnp.float32) for n in (width, HIGH, LOW)]
    own, first, last = pl.pallas_call(
        prepare_kernel,
        out_shape=rows,
        in_specs=[vmem],
        out_specs=[vmem] * 3,
        compiler_params=limit,
    )(permeability)
    tiles = (own, ring(last, "gx", 1), high, ring(first, "gx", -2))
    tiles = tuple(pltpu.with_memory_space_constraint(t, pltpu.VMEM) for t in tiles)
    packed = pl.pallas_call(
        pack_kernel,
        out_shape=pltpu.VMEM((-(-count // per), depth, lanes), jnp.float32),
        in_specs=[vmem] * 4,
        out_specs=vmem,
        compiler_params=limit,
    )(*tiles)
    even = pltpu.with_memory_space_constraint(swap(packed, ("gx", "gy"), 0), pltpu.VMEM)
    odd = pltpu.with_memory_space_constraint(swap(packed, ("gx", "gy"), 1), pltpu.VMEM)
    scratch = [pltpu.VMEM((256, depth, lanes), jnp.float32)]
    inner = pl.pallas_call(
        main_kernel,
        out_shape=pltpu.VMEM((8 * NCL, lanes), jnp.float32),
        compiler_params=limit,
        in_specs=[smem] + [vmem] * 4,
        out_specs=vmem,
        scratch_shapes=scratch,
        cost_estimate=pl.CostEstimate(flops=6_000_000, bytes_accessed=4 * permeability.size * 4, transcendentals=0),
    )(layer_map, *tiles)
    out = jax.ShapeDtypeStruct((3, NCL, width // BXY, lanes // BXY), jnp.float32)
    return pl.pallas_call(
        edge_kernel,
        out_shape=(out, out),
        in_specs=[smem] + [vmem] * 7,
        out_specs=(vmem, vmem),
        compiler_params=limit,
        scratch_shapes=scratch,
    )(layer_map, *tiles, even, odd, pltpu.with_memory_space_constraint(inner, pltpu.VMEM))


def solution(mesh):
    in_specs = (P(None, None, "gx", "gy"), P())
    out_specs = (P(None, None, "gx", "gy"), P(None, None, "gx", "gy"))
    return jax.shard_map(local, mesh=mesh, in_specs=in_specs, out_specs=out_specs, check_vma=False)
```

```python
import functools
import math

import jax
import jax.numpy as jnp
from jax import lax
from jax.experimental import pallas as pl
from jax.experimental.pallas import tpu as pltpu
from jax.sharding import PartitionSpec as P

NCL = 4
BXY = 8
SWEEPS = 4
KMIN = 0.01
EPS = 1e-06

LOW = SWEEPS
HIGH = SWEEPS + 1
RIGHT = BXY + HIGH
SLOT = LOW + RIGHT


def sweep_weights(count):
    return [
        1.0 / (1.05 + 0.95 * math.cos(math.pi * (2 * s + 1) / (2 * count))) for s in range(count)
    ]


WEIGHTS = sweep_weights(SWEEPS)


def harmonic(left, right):
    return 2.0 * left * right / (left + right)


def lanes_of(shape):
    return lax.broadcasted_iota(jnp.int32, shape, len(shape) - 1)


def up(value, axis):
    return pltpu.roll(value, value.shape[axis] - 1, axis)


def down(value, axis):
    return pltpu.roll(value, 1, axis)


def layers_of(tile, comp, row):
    _, depth, width, lanes = tile.shape
    flat = tile.reshape(3 * depth * width, lanes)
    return flat[pl.ds(comp * depth * width + row, depth, stride=width), :]


LONG = 10**10


class Solver:
    def __init__(self, perm, scratch, y_ends, y_starts):
        self.perm_of = perm
        self.scratch = scratch
        self.slots = {}
        self.cache = {}
        shape = scratch.shape[1:]
        layer = lax.broadcasted_iota(jnp.int32, shape, 0)
        self.top = layer == shape[0] - 1
        self.bottom = layer == 0
        self.y_ends = y_ends
        self.y_starts = y_starts

    def memo(self, key, make):
        if key not in self.cache:
            self.cache[key] = make()
        return self.cache[key]

    def stored(self, key, make):
        if key not in self.slots:
            values = make()
            base = sum(n for _, n in self.slots.values())
            self.slots[key] = (base, len(values))
            for i, value in enumerate(values):
                self.scratch[base + i] = value
        base, _ = self.slots[key]
        return lambda i: self.scratch[base + i]

    def perm(self, comp, row):
        return self.memo(("k", comp, row), lambda: self.perm_of(comp, row))

    def tx(self, row):
        return self.memo(("tx", row), lambda: harmonic(self.perm(0, row), self.perm(0, row + 1)))

    def tyz(self, row):
        def make():
            ky, kz = self.perm(1, row), self.perm(2, row)
            ty = harmonic(ky, up(ky, 1))
            if self.y_ends is not None:
                ty = jnp.where(self.y_ends, ky, ty)
            ty_low = down(ty, 1)
            if self.y_starts is not None:
                ty_low = jnp.where(self.y_starts, ky, ty_low)
            tz = jnp.where(self.top, kz, harmonic(kz, up(kz, 0)))
            tz_low = jnp.where(self.bottom, kz, down(tz, 0))
            return ty, ty_low, tz, tz_low

        return self.memo(("tyz", row), make)

    def faces(self, row, edge):
        upper = self.perm(0, row) if edge == "up" else self.tx(row)
        lower = self.perm(0, row) if edge == "low" else self.tx(row - 1)
        return upper, lower

    def edge_of(self, row, boundary):
        return boundary[0] if boundary is not None and boundary[1] == row else None

    def coefficients(self, row, boundary):
        edge = self.edge_of(row, boundary)

        def make():
            upper, lower = self.faces(row, edge)
            ty, ty_low, tz, tz_low = self.tyz(row)
            inverse = 1.0 / (((upper + lower) + (ty + ty_low)) + (tz + tz_low))
            zero = jnp.zeros_like(inverse)
            ax = zero if edge == "up" else upper * inverse
            ax_low = zero if edge == "low" else lower * inverse
            ay, ay_low = ty * inverse, ty_low * inverse
            az, az_low = tz * inverse, tz_low * inverse
            drive = ((upper - lower) * inverse, ay - ay_low, az - az_low)
            if self.y_ends is not None:
                ay = jnp.where(self.y_ends, 0.0, ay)
            if self.y_starts is not None:
                ay_low = jnp.where(self.y_starts, 0.0, ay_low)
            az = jnp.where(self.top, 0.0, az)
            az_low = jnp.where(self.bottom, 0.0, az_low)
            return (ax, ax_low, ay, ay_low, az, az_low) + drive

        return self.stored(("c", row, edge), make)

    def pressure(self, d, count, row, boundary):
        if boundary is not None:
            _, at = boundary
            if abs(row - at) >= count:
                boundary = None

        def make():
            c = self.coefficients(row, boundary)
            edge = self.edge_of(row, boundary)
            if count == 1:
                return WEIGHTS[0] * c(6 + d)
            here = self.pressure(d, count - 1, row, boundary)
            total = c(6 + d)
            if edge != "up":
                total = total + c(0) * self.pressure(d, count - 1, row + 1, boundary)
            if edge != "low":
                total = total + c(1) * self.pressure(d, count - 1, row - 1, boundary)
            side = c(2) * up(here, 1) + c(3) * down(here, 1)
            total = total + side
            total = total + (c(4) * up(here, 0) + c(5) * down(here, 0))
            return here + WEIGHTS[count - 1] * (total - here)

        return self.memo(("u", d, count, row, boundary), make)

    def sums(self, d, row, boundary):
        if boundary is not None:
            kind, at = boundary
            reach = SWEEPS + (1 if d == 0 and kind == "up" else 0)
            if abs(row - at) >= reach:
                boundary = None

        def make():
            here = self.pressure(d, SWEEPS, row, boundary)
            edge = self.edge_of(row, boundary)
            if d == 0:
                face = self.faces(row, edge)[0]
                above = None if edge == "up" else self.pressure(d, SWEEPS, row + 1, boundary)
            elif d == 1:
                face = self.tyz(row)[0]
                above = up(here, 1)
                if self.y_ends is not None:
                    above = jnp.where(self.y_ends, 0.0, above)
            else:
                face = self.tyz(row)[2]
                above = jnp.where(self.top, 0.0, up(here, 0))
            drop = (1.0 - here) if above is None else (1.0 - here) + above
            square = drop * drop
            return face * square, square

        return self.memo(("s", d, row, boundary), make)

    def block(self, d, begin, patches):
        groups = {}
        for row in range(begin, begin + BXY):
            for boundary, weight in patches:
                pair = self.sums(d, row, boundary)
                groups.setdefault(id(weight), (weight, []))[1].append(pair)
        totals = None
        for weight, pairs in groups.values():
            part = [functools.reduce(jnp.add, parts) for parts in zip(*pairs)]
            if weight is not None:
                part = [weight * p for p in part]
            totals = part if totals is None else [a + b for a, b in zip(totals, part)]
        return totals


def accumulate(solver, present):
    low, high, high2 = present
    own = [(("up", BXY - 1), low), (None, None), (("low", 0), high)]
    after = [(("up", 2 * BXY - 1), None), (None, None), (("low", BXY), high2)]
    jobs = [(d, 0, own) for d in range(3)] + [(0, BXY, after)]
    results = {}
    order = [jobs[0], jobs[1], jobs[2], jobs[3]]
    for row in range(BXY):
        for d, begin, patches in order:
            for boundary, _ in patches:
                solver.sums(d, begin + row, boundary)
    for i, (d, begin, patches) in enumerate(jobs):
        results[i] = solver.block(d, begin, patches)
    return [value for i in range(len(jobs)) for value in results[i]]


def sum_columns(sums, columns):
    return jnp.dot(
        jnp.concatenate(sums, axis=0),
        columns,
        precision=lax.Precision.HIGHEST,
        preferred_element_type=jnp.float32,
    )


def picks_kernel(layer_map, out):
    depth = out.shape[1] // (out.shape[0] // NCL)
    r = lax.broadcasted_iota(jnp.int32, out.shape, 0)
    c = lax.broadcasted_iota(jnp.int32, out.shape, 1)
    layer = jnp.zeros(out.shape, jnp.int32)
    for z in range(depth):
        layer = jnp.where(c % depth == z, layer_map[z], layer)
    out[...] = ((r // NCL == c // depth) & (r % NCL == layer)).astype(jnp.float32)


def place(axes):
    i, j = (lax.axis_index(a) for a in axes)
    nx, ny = (lax.axis_size(a) for a in axes)
    core, chip = i % 2, i // 2
    one = lambda test: jnp.where(test, 1.0, 0.0).astype(jnp.float32)
    tiles = one(i > 0), one(i < nx - 1), one(i < nx - 2)
    chips = one(chip > 0), one(chip < nx // 2 - 1)
    return core, tiles, chips, (one(j > 0), one(j < ny - 1))


def slots(width):
    return [(comp, row) for row in range(width) for comp in range(3)]


def table_kernel(out):
    lanes = out.shape[0]
    r = lax.broadcasted_iota(jnp.int32, out.shape, 0)
    c = lax.broadcasted_iota(jnp.int32, out.shape, 1)
    inner = (r // BXY == c) & (c > 0) & (c < lanes // BXY - 1)
    out[...] = inner.astype(jnp.float32)


def pack_kernel(mine, other, pair, packed):
    core, _, _, _ = place(("gx", "gy"))
    _, depth, width, lanes = mine.shape
    per = lanes // SLOT
    lane = lanes_of((depth, lanes))
    rows = slots(width)
    count = packed.shape[0] // 2
    for tile, at in ((mine, core), (other, 1 - core)):
        strip = None
        for n, (comp, row) in enumerate(rows):
            value = layers_of(tile, comp, row)
            pair[at * width + row, comp] = value
            slot = n % per
            value = pltpu.roll(value, (LOW + SLOT * slot) % lanes, 1)
            strip = value if slot == 0 else jnp.where(lane < SLOT * slot, strip, value)
            if slot == per - 1 or n == len(rows) - 1:
                packed[at * count + n // per] = strip


def join_kernel(below, beside, above, out):
    half = beside.shape[0] // 2
    out[:half] = below[half:]
    out[half : 3 * half] = beside[...]
    out[3 * half :] = above[...]


def main_kernel(columns, pair, up_mine, up_other, down_mine, down_other, out, stack, scratch):
    core, present, (has_down, has_up), _ = place(("gx", "gy"))
    width = up_mine.shape[2]
    for row in range(2 * width):
        for comp in range(3):
            stack[LOW + row, comp] = pair[row, comp] + KMIN
    first = core == 0
    for row in range(width):
        for comp in range(3):
            mine, other = layers_of(up_mine, comp, row), layers_of(up_other, comp, row)
            above = LOW + 2 * width + row
            stack[above, comp] = jnp.where(first, mine, other) * has_up + KMIN
            if row < HIGH:
                stack[above + width, comp] = jnp.where(first, other, mine) * has_up + KMIN
            if row >= width - LOW:
                if down_mine is not up_mine:
                    mine, other = layers_of(down_mine, comp, row), layers_of(down_other, comp, row)
                low = jnp.where(first, other, mine) * has_down + KMIN
                stack[row - width + LOW, comp] = low
    base = LOW + core * width
    solver = Solver(lambda comp, row: stack[base + row, comp], scratch, None, None)
    out[...] = sum_columns(accumulate(solver, present), columns[...])


def edge_kernel(picks, stack, mine, other, inner, perm_out, trans_out, strips, scratch):
    core, present, (has_down, has_up), (has_left, has_right) = place(("gx", "gy"))
    depth, lanes = stack.shape[2:]
    width = BXY
    per = lanes // SLOT
    lane = lanes_of((depth, lanes))
    half = lanes // 2
    left = RIGHT + 7
    start = left + LOW
    stop = start + BXY + HIGH
    in_left = lane % SLOT < LOW
    from_mine = in_left == (jnp.zeros_like(lane) + core == 1)
    keep = jnp.where(in_left, has_left, has_right)
    per_tile = strips.shape[0] // 5
    for at in range(strips.shape[0]):
        there = has_down if at < per_tile else None if at < 3 * per_tile else has_up
        weight = keep if there is None else keep * there
        strips[at] = jnp.where(from_mine, mine[at], other[at]) * weight + KMIN

    index = {key: at for at, key in enumerate(slots(width))}
    second = (lane >= half - BXY - LOW) & (lane < half + stop)
    base = LOW + core * width

    def perm(comp, row):
        at = index[comp, row % width]
        slot = at % per
        own = stack[base + row, comp]
        theirs = strips[(core + 1 + row // width) * per_tile + at // per]
        right = pltpu.roll(theirs, (-(SLOT * slot + LOW)) % lanes, 1)
        before = pltpu.roll(theirs, (left - SLOT * slot) % lanes, 1)
        value = jnp.where(lane < RIGHT, right, own)
        value = jnp.where((lane >= left) & (lane < stop), pltpu.roll(own, start, 1), value)
        value = jnp.where((lane >= left) & (lane < start), before, value)
        return jnp.where(second, pltpu.roll(value, half, 1), value)

    y_ends = (lane == BXY - 1) | (lane == half + start + BXY - 1)
    y_starts = lane == half - BXY
    solver = Solver(perm, scratch, y_ends, y_starts)
    sums = accumulate(solver, present)
    r = lax.broadcasted_iota(jnp.int32, (lanes, lanes), 0)
    c = lax.broadcasted_iota(jnp.int32, (lanes, lanes), 1)
    count = lanes // BXY

    def span(begin):
        return (r >= begin) & (r < begin + BXY)

    first = jnp.where(span(start), 1.0, 0.0) + jnp.where(span(half + start), has_left, 0.0)
    final = jnp.where(span(lanes - BXY), 1.0, 0.0) + jnp.where(span(half - BXY), has_right, 0.0)
    beyond = jnp.where(span(0) | span(half), has_right, 0.0)
    columns = jnp.where(
        c == 0, first, jnp.where(c == count - 1, final, jnp.where(c == count, beyond, 0.0))
    )
    total = jnp.dot(
        picks[...],
        inner[...] + sum_columns(sums, columns),
        precision=lax.Precision.HIGHEST,
        preferred_element_type=jnp.float32,
    )
    cells = (width + 2 * BXY, lanes + 2 * BXY, depth)
    energy = [total[2 * NCL * q : 2 * NCL * q + NCL] for q in range(4)]
    square = [total[2 * NCL * q + NCL : 2 * NCL * (q + 1)] for q in range(4)]
    perms = [
        energy[q] / (square[q] + EPS * float(cells[d]) ** 2) for q, d in enumerate((0, 1, 2, 0))
    ]
    layer = lax.broadcasted_iota(jnp.int32, perms[0].shape, 0)
    trans = [
        harmonic(perms[0], perms[3] * present[1]),
        harmonic(perms[1], up(perms[1], 1)),
    ]
    above = jnp.concatenate([perms[2][1:], jnp.zeros_like(perms[2][:1])], axis=0)
    trans.append(harmonic(perms[2], above))
    for d in range(3):
        for l in range(NCL):
            perm_out[d, l, :, :] = perms[d][l : l + 1, :count]
            trans_out[d, l, :, :] = trans[d][l : l + 1, :count]


class Exchange:
    def __init__(self, axes):
        self.axes = axes
        self.nx, self.ny = (lax.axis_size(a) for a in axes)
        self.sent = {}

    def permute(self, value, target):
        nx, ny = self.nx, self.ny
        pairs = []
        for i in range(nx):
            for j in range(ny):
                a, b = target(i, j)
                pairs.append((i * ny + j, a % nx * ny + b))
        key = (id(value), tuple(pairs))
        if key not in self.sent:
            self.sent[key] = (value, lax.ppermute(value, self.axes, pairs))
        return self.sent[key][1]

    def swap(self, value):
        return self.permute(value, lambda i, j: (i ^ 1, j))

    def straight(self, value, pairs):
        return self.permute(value, lambda i, j: (i - 2 * pairs, j))

    def sideways(self, value, pairs):
        def target(i, j):
            to = j - 1 if i % 2 == 0 else j + 1
            i -= 2 * pairs
            return (i, to) if 0 <= to < self.ny else (i ^ 1, j)

        return self.permute(value, target)


def local(permeability, layer_map):
    _, depth, width, lanes = permeability.shape
    net = Exchange(("gx", "gy"))
    if width != BXY or depth != 8 or lanes != 128 or net.nx % 2:
        raise ValueError("unsupported tile")
    vmem = pl.BlockSpec(memory_space=pltpu.VMEM)
    smem = pl.BlockSpec(memory_space=pltpu.SMEM)
    limit = pltpu.CompilerParams(vmem_limit_bytes=16 << 20)
    held = lambda value: pltpu.with_memory_space_constraint(value, pltpu.VMEM)
    strips = -(-len(slots(width)) // (lanes // SLOT))

    columns = pl.pallas_call(
        table_kernel,
        out_shape=pltpu.VMEM((lanes, lanes), jnp.float32),
        out_specs=vmem,
        compiler_params=limit,
        cost_estimate=pl.CostEstimate(flops=LONG, bytes_accessed=lanes * lanes * 4, transcendentals=0),
    )()
    other = net.swap(permeability)
    up, down = net.straight(permeability, 1), net.straight(permeability, -1)
    pair, packed = pl.pallas_call(
        pack_kernel,
        out_shape=[
            pltpu.VMEM((2 * width, 3, depth, lanes), jnp.float32),
            pltpu.VMEM((2 * strips, depth, lanes), jnp.float32),
        ],
        in_specs=[vmem] * 2,
        out_specs=[vmem] * 2,
        compiler_params=limit,
    )(held(permeability), held(other))
    above, below = net.sideways(packed, 1), net.sideways(packed, -1)
    beside = net.sideways(packed, 0)
    up_other, down_other = net.swap(up), net.swap(down)
    picks = pl.pallas_call(
        picks_kernel,
        out_shape=pltpu.VMEM((8 * NCL, 8 * depth), jnp.float32),
        in_specs=[smem],
        out_specs=vmem,
        compiler_params=limit,
    )(layer_map)
    scratch = pltpu.VMEM((256, depth, lanes), jnp.float32)
    inner, stack = pl.pallas_call(
        main_kernel,
        out_shape=[
            pltpu.VMEM((8 * depth, lanes), jnp.float32),
            pltpu.VMEM((LOW + 3 * width + HIGH, 3, depth, lanes), jnp.float32),
        ],
        in_specs=[vmem] * 6,
        out_specs=[vmem] * 2,
        scratch_shapes=[scratch],
        compiler_params=limit,
        cost_estimate=pl.CostEstimate(flops=LONG, bytes_accessed=4 * permeability.size * 4, transcendentals=0),
    )(held(columns), held(pair), held(up), held(up_other), held(down), held(down_other))
    joined = pl.pallas_call(
        join_kernel,
        out_shape=pltpu.VMEM((5 * strips, depth, lanes), jnp.float32),
        in_specs=[vmem] * 3,
        out_specs=vmem,
        compiler_params=limit,
    )(held(below), held(beside), held(above))
    theirs = net.swap(joined)
    out = jax.ShapeDtypeStruct((3, NCL, width // BXY, lanes // BXY), jnp.float32)
    return pl.pallas_call(
        edge_kernel,
        out_shape=(out, out),
        in_specs=[vmem] * 5,
        out_specs=(vmem, vmem),
        scratch_shapes=[pltpu.VMEM((5 * strips, depth, lanes), jnp.float32), scratch],
        compiler_params=limit,
    )(held(picks), held(stack), held(joined), held(theirs), held(inner))


def solution(mesh):
    in_specs = (P(None, None, "gx", "gy"), P())
    out_specs = (P(None, None, "gx", "gy"), P(None, None, "gx", "gy"))
    return jax.shard_map(local, mesh=mesh, in_specs=in_specs, out_specs=out_specs, check_vma=False)
```

```python
import functools
import math

import jax
import jax.numpy as jnp
from jax import lax
from jax.experimental import pallas as pl
from jax.experimental.pallas import tpu as pltpu
from jax.sharding import PartitionSpec as P

NCL = 4
BXY = 8
SWEEPS = 4
KMIN = 0.01
EPS = 1e-06

LOW = SWEEPS
HIGH = SWEEPS + 1
RIGHT = BXY + HIGH
START = RIGHT + LOW


def sweep_weights(count):
    return [
        1.0 / (1.05 + 0.95 * math.cos(math.pi * (2 * s + 1) / (2 * count))) for s in range(count)
    ]


WEIGHTS = sweep_weights(SWEEPS)


SCALES = [math.prod(WEIGHTS[: s + 1]) for s in range(SWEEPS)]


def harmonic(left, right):
    return 2.0 * left * right / (left + right)


def lanes_of(shape):
    return lax.broadcasted_iota(jnp.int32, shape, len(shape) - 1)


def up(value, axis):
    return pltpu.roll(value, value.shape[axis] - 1, axis)


def down(value, axis):
    return pltpu.roll(value, 1, axis)


def layers_of(tile, comp, row):
    _, depth, width, lanes = tile.shape
    flat = tile.reshape(3 * depth * width, lanes)
    return flat[pl.ds(comp * depth * width + row, depth, stride=width), :]


LONG = 10**10


class Solver:
    def __init__(self, inverse_of, scratch, y_ends, y_starts):
        self.inverse_of = inverse_of
        self.scratch = scratch
        self.slots = {}
        self.cache = {}
        shape = scratch.shape[1:]
        layer = lax.broadcasted_iota(jnp.int32, shape, 0)
        self.top = layer == shape[0] - 1
        self.bottom = layer == 0
        self.y_ends = y_ends
        self.y_starts = y_starts

    def memo(self, key, make):
        if key not in self.cache:
            self.cache[key] = make()
        return self.cache[key]

    def stored(self, key, make):
        if key not in self.slots:
            value = make()
            self.slots[key] = len(self.slots)
            self.scratch[self.slots[key]] = value
        return self.scratch[self.slots[key]]

    def inverse(self, comp, row):
        return self.memo(("k", comp, row), lambda: self.inverse_of(comp, row))

    def x_face(self, row):
        return self.memo(("tx", row), lambda: 1.0 / (self.inverse(0, row) + self.inverse(0, row + 1)))

    def x_edge(self, row):
        return self.memo(("te", row), lambda: 1.0 / (self.inverse(0, row) + self.inverse(0, row)))

    def y_faces(self, row):
        def make():
            here = self.inverse(1, row)
            above = up(here, 1)
            if self.y_ends is None:
                upper = 1.0 / (here + above)
                return upper, down(upper, 1)
            below = jnp.where(self.y_starts, here, down(here, 1))
            return 1.0 / (here + jnp.where(self.y_ends, here, above)), 1.0 / (here + below)

        return self.memo(("ty", row), make)

    def z_faces(self, row):
        def make():
            here = self.inverse(2, row)
            above = jnp.where(self.top, here, up(here, 0))
            below = jnp.where(self.bottom, here, down(here, 0))
            return 1.0 / (here + above), 1.0 / (here + below)

        return self.memo(("tz", row), make)

    def side_faces(self, row):
        def make():
            ty, ty_low = self.y_faces(row)
            tz, tz_low = self.z_faces(row)
            total = (ty + ty_low) + (tz + tz_low)
            if self.y_ends is not None:
                ty = jnp.where(self.y_ends, 0.0, ty)
                ty_low = jnp.where(self.y_starts, 0.0, ty_low)
            return ty, ty_low, jnp.where(self.top, 0.0, tz), jnp.where(self.bottom, 0.0, tz_low), total

        return self.memo(("side", row), make)

    def x_faces(self, row, edge):
        upper = self.x_edge(row) if edge == "up" else self.x_face(row)
        lower = self.x_edge(row) if edge == "low" else self.x_face(row - 1)
        return upper, lower

    def edge_of(self, row, boundary):
        return boundary[0] if boundary is not None and boundary[1] == row else None

    def scale(self, row, edge):
        def make():
            upper, lower = self.x_faces(row, edge)
            return 1.0 / ((upper + lower) + self.side_faces(row)[4])

        return self.memo(("h", row, edge), make)

    def weight(self, which, row, edge):
        def make():
            faces = self.x_faces(row, edge) if which < 2 else self.side_faces(row)[:4]
            return faces[which % 2 if which < 2 else which - 2] * self.scale(row, edge)

        return self.stored(("a", which, row, edge), make)

    def drive(self, d, row, edge):
        def make():
            upper, lower = (
                self.x_faces(row, edge) if d == 0 else self.y_faces(row) if d == 1 else self.z_faces(row)
            )
            return (upper - lower) * self.scale(row, edge)

        return self.stored(("c", d, row, edge), make)

    def pressure(self, d, count, row, boundary):
        if boundary is not None and abs(row - boundary[1]) >= count:
            boundary = None
        edge = self.edge_of(row, boundary)
        if count == 1:
            return self.drive(d, row, edge)

        def make():
            a = lambda which: self.weight(which, row, edge)
            here = self.pressure(d, count - 1, row, boundary)
            w = WEIGHTS[count - 1]
            if count == 2:
                total = ((1.0 - w) / w + 1.0 / SCALES[0]) * here
            else:
                total = ((1.0 - w) / w) * here + (1.0 / SCALES[count - 2]) * self.drive(d, row, edge)
            side = a(2) * up(here, 1) + a(3) * down(here, 1)
            layers = a(4) * up(here, 0) + a(5) * down(here, 0)
            if edge != "up":
                total = total + a(0) * self.pressure(d, count - 1, row + 1, boundary)
            if edge != "low":
                total = total + a(1) * self.pressure(d, count - 1, row - 1, boundary)
            return total + (side + layers)

        return self.memo(("u", d, count, row, boundary), make)

    def sums(self, d, row, boundary):
        if boundary is not None:
            reach = SWEEPS + (1 if d == 0 and boundary[0] == "up" else 0)
            if abs(row - boundary[1]) >= reach:
                boundary = None

        def make():
            here = self.pressure(d, SWEEPS, row, boundary)
            edge = self.edge_of(row, boundary)
            if d == 0:
                face = self.x_faces(row, edge)[0]
                above = None if edge == "up" else self.pressure(d, SWEEPS, row + 1, boundary)
            elif d == 1:
                face = self.y_faces(row)[0]
                above = up(here, 1)
                if self.y_ends is not None:
                    above = jnp.where(self.y_ends, 0.0, above)
            else:
                face = self.z_faces(row)[0]
                above = jnp.where(self.top, 0.0, up(here, 0))
            drop = 1.0 / SCALES[-1] - here
            if above is not None:
                drop = drop + above
            square = drop * drop
            return face * square, square

        return self.memo(("s", d, row, boundary), make)

    def block(self, d, begin, patches):
        uses = {}
        for row in range(begin, begin + BXY):
            for boundary, weight in patches:
                pair = self.sums(d, row, boundary)
                uses.setdefault(id(pair), (pair, []))[1].append(weight)
        groups = {}
        for pair, weights in uses.values():
            groups.setdefault(tuple(map(id, weights)), (weights, []))[1].append(pair)
        totals = None
        for weights, pairs in groups.values():
            part = [functools.reduce(jnp.add, parts) for parts in zip(*pairs)]
            if weights != [None]:
                factor = sum(1.0 if w is None else w for w in weights)
                part = [factor * p for p in part]
            totals = part if totals is None else [a + b for a, b in zip(totals, part)]
        return totals


def accumulate(solver, present):
    low, high, high2 = present
    own = [(("up", BXY - 1), low), (None, None), (("low", 0), high)]
    after = [(("up", 2 * BXY - 1), None), (None, None), (("low", BXY), high2)]
    jobs = [(d, 0, own) for d in range(3)] + [(0, BXY, after)]
    results = {}
    order = [jobs[0], jobs[1], jobs[2], jobs[3]]
    for row in range(BXY):
        for d, begin, patches in order:
            for boundary, _ in patches:
                solver.sums(d, begin + row, boundary)
    for i, (d, begin, patches) in enumerate(jobs):
        results[i] = solver.block(d, begin, patches)
    return [value for i in range(len(jobs)) for value in results[i]]


def thirds(value):
    parts = []
    for _ in range(3):
        parts.append(value.astype(jnp.bfloat16))
        value = value - parts[-1].astype(jnp.float32)
    return parts


def sum_columns(sums, columns):
    value = jnp.concatenate(sums, axis=0)
    count = value.shape[0]
    parts = jnp.dot(
        jnp.concatenate(thirds(value), axis=0),
        columns.astype(jnp.bfloat16),
        preferred_element_type=jnp.float32,
    )
    return parts[:count] + parts[count : 2 * count] + parts[2 * count :]


def sum_layers(picks, value):
    return jnp.dot(
        jnp.concatenate([picks.astype(jnp.bfloat16)] * 3, axis=1),
        jnp.concatenate(thirds(value), axis=0),
        preferred_element_type=jnp.float32,
    )


def picks_kernel(layer_map, out):
    depth = out.shape[1] // (out.shape[0] // NCL)
    r = lax.broadcasted_iota(jnp.int32, out.shape, 0)
    c = lax.broadcasted_iota(jnp.int32, out.shape, 1)
    layer = jnp.zeros(out.shape, jnp.int32)
    for z in range(depth):
        layer = jnp.where(c % depth == z, layer_map[z], layer)
    out[...] = ((r // NCL == c // depth) & (r % NCL == layer)).astype(jnp.float32)


def place(axes):
    i, j = (lax.axis_index(a) for a in axes)
    nx, ny = (lax.axis_size(a) for a in axes)
    core, chip = i % 2, i // 2
    one = lambda test: jnp.where(test, 1.0, 0.0).astype(jnp.float32)
    tiles = one(i > 0), one(i < nx - 1), one(i < nx - 2)
    chips = one(chip > 0), one(chip < nx // 2 - 1)
    return core, tiles, chips, (one(j > 0), one(j < ny - 1))


def slots(width):
    return [(comp, row) for row in range(width) for comp in range(3)]


def table_kernel(out):
    lanes = out.shape[0]
    r = lax.broadcasted_iota(jnp.int32, out.shape, 0)
    c = lax.broadcasted_iota(jnp.int32, out.shape, 1)
    inner = (r // BXY == c) & (c > 0) & (c < lanes // BXY - 1)
    out[...] = inner.astype(jnp.float32)


def pack_kernel(mine, other, pair, packed):
    core, _, _, _ = place(("gx", "gy"))
    _, depth, width, lanes = mine.shape
    per = lanes // RIGHT
    lane = lanes_of((depth, lanes))
    rows = slots(width)
    count = packed.shape[0] // 2
    for tile, at in ((mine, core), (other, 1 - core)):
        strip = None
        for n, (comp, row) in enumerate(rows):
            value = layers_of(tile, comp, row)
            pair[at * width + row, comp] = value
            shift = RIGHT * (n % per)
            value = pltpu.roll(value, shift + core * START, 1)
            strip = value if n % per == 0 else jnp.where(lane < shift + core * RIGHT, strip, value)
            if n % per == per - 1 or n == len(rows) - 1:
                packed[at * count + n // per] = strip


def join_kernel(below, beside, above, out):
    half = beside.shape[0] // 2
    out[:half] = below[half:]
    out[half : 3 * half] = beside[...]
    out[3 * half :] = above[...]


def stack_kernel(pair, up_mine, up_other, down_mine, down_other, stack, placed):
    core, _, (has_down, has_up), _ = place(("gx", "gy"))
    width = up_mine.shape[2]
    depth, lanes = pair.shape[2:]
    first = core == 0
    lane = lanes_of((depth, lanes))
    half, start = lanes // 2, START
    stop = start + BXY + HIGH
    near = (lane >= start) & (lane < stop)
    second = (lane >= half - BXY - LOW) & (lane < half + stop)

    def put(row, comp, value):
        value = 1.0 / (value + KMIN)
        stack[LOW + row, comp] = value
        value = jnp.where(near, pltpu.roll(value, start, 1), value)
        placed[LOW + row, comp] = jnp.where(second, pltpu.roll(value, half, 1), value)

    for row in range(2 * width):
        for comp in range(3):
            put(row, comp, pair[row, comp])
    for row in range(width):
        for comp in range(3):
            mine, other = layers_of(up_mine, comp, row), layers_of(up_other, comp, row)
            put(2 * width + row, comp, jnp.where(first, mine, other) * has_up)
            if row < HIGH:
                put(3 * width + row, comp, jnp.where(first, other, mine) * has_up)
            if row >= width - LOW:
                mine, other = layers_of(down_mine, comp, row), layers_of(down_other, comp, row)
                put(row - width, comp, jnp.where(first, other, mine) * has_down)


def main_kernel(columns, stack, out, scratch):
    core, present, _, _ = place(("gx", "gy"))
    base = LOW + core * BXY
    solver = Solver(lambda comp, row: stack[base + row, comp], scratch, None, None)
    out[...] = sum_columns(accumulate(solver, present), columns[...])


def edge_kernel(picks, placed, mine, other, inner, perm_out, trans_out, scratch):
    core, present, _, (has_left, has_right) = place(("gx", "gy"))
    depth, lanes = placed.shape[2:]
    width = BXY
    per = lanes // RIGHT
    lane = lanes_of((depth, lanes))
    half, start = lanes // 2, START
    first = core == 0
    low, high, high2 = present
    kept = {-1: low, 0: 1.0, 1: high, 2: high2}
    per_tile = mine.shape[0] // 5
    index = {key: at for at, key in enumerate(slots(width))}
    turned = (lane >= half) & (lane < half + START)
    strips = {}

    def strip(tile, n):
        if (tile, n) not in strips:
            at = (core + 1 + tile) * per_tile + n
            a, b = mine[at], other[at]
            strips[tile, n] = tuple(
                1.0 / (value * (kept[tile] * there) + KMIN)
                for value, there in ((jnp.where(first, a, b), has_right), (jnp.where(first, b, a), has_left))
            )
        return strips[tile, n]

    base = LOW + core * width

    def inverse(comp, row):
        at = index[comp, row % width]
        shift = -RIGHT * (at % per) % lanes
        right, left = (pltpu.roll(v, shift, 1) if shift else v for v in strip(row // width, at // per))
        theirs = jnp.where(lane < RIGHT, right, left)
        value = jnp.where(turned, pltpu.roll(theirs, half, 1), placed[base + row, comp])
        return jnp.where(lane < START, theirs, value)

    y_ends = (lane == BXY - 1) | (lane == half + start + BXY - 1)
    y_starts = lane == half - BXY
    solver = Solver(inverse, scratch, y_ends, y_starts)
    sums = accumulate(solver, present)
    r = lax.broadcasted_iota(jnp.int32, (lanes, lanes), 0)
    c = lax.broadcasted_iota(jnp.int32, (lanes, lanes), 1)
    count = lanes // BXY

    def span(begin):
        return (r >= begin) & (r < begin + BXY)

    first = jnp.where(span(start), 1.0, 0.0) + jnp.where(span(half + start), has_left, 0.0)
    final = jnp.where(span(lanes - BXY), 1.0, 0.0) + jnp.where(span(half - BXY), has_right, 0.0)
    beyond = jnp.where(span(0) | span(half), has_right, 0.0)
    columns = jnp.where(
        c == 0, first, jnp.where(c == count - 1, final, jnp.where(c == count, beyond, 0.0))
    )
    total = sum_layers(picks[...], inner[...] + sum_columns(sums, columns))
    cells = (width + 2 * BXY, lanes + 2 * BXY, depth)
    energy = [total[2 * NCL * q : 2 * NCL * q + NCL] for q in range(4)]
    square = [total[2 * NCL * q + NCL : 2 * NCL * (q + 1)] for q in range(4)]
    perms = [
        2.0 * energy[q] / (square[q] + EPS * (cells[d] / SCALES[-1]) ** 2)
        for q, d in enumerate((0, 1, 2, 0))
    ]
    layer = lax.broadcasted_iota(jnp.int32, perms[0].shape, 0)
    trans = [
        harmonic(perms[0], perms[3] * present[1]),
        harmonic(perms[1], up(perms[1], 1)),
    ]
    above = jnp.concatenate([perms[2][1:], jnp.zeros_like(perms[2][:1])], axis=0)
    trans.append(harmonic(perms[2], above))
    for d in range(3):
        for l in range(NCL):
            perm_out[d, l, :, :] = perms[d][l : l + 1, :count]
            trans_out[d, l, :, :] = trans[d][l : l + 1, :count]


class Exchange:
    def __init__(self, axes):
        self.axes = axes
        self.nx, self.ny = (lax.axis_size(a) for a in axes)
        self.sent = {}

    def permute(self, value, target):
        nx, ny = self.nx, self.ny
        pairs = []
        for i in range(nx):
            for j in range(ny):
                a, b = target(i, j)
                pairs.append((i * ny + j, a % nx * ny + b))
        key = (id(value), tuple(pairs))
        if key not in self.sent:
            self.sent[key] = (value, lax.ppermute(value, self.axes, pairs))
        return self.sent[key][1]

    def swap(self, value):
        return self.permute(value, lambda i, j: (i ^ 1, j))

    def straight(self, value, pairs):
        return self.permute(value, lambda i, j: (i - 2 * pairs, j))

    def sideways(self, value, pairs):
        def target(i, j):
            to = j - 1 if i % 2 == 0 else j + 1
            i -= 2 * pairs
            return (i, to) if 0 <= to < self.ny else (i ^ 1, j)

        return self.permute(value, target)


def local(permeability, layer_map):
    _, depth, width, lanes = permeability.shape
    net = Exchange(("gx", "gy"))
    if width != BXY or depth != 8 or lanes != 128 or net.nx % 2:
        raise ValueError("unsupported tile")
    vmem = pl.BlockSpec(memory_space=pltpu.VMEM)
    smem = pl.BlockSpec(memory_space=pltpu.SMEM)
    limit = pltpu.CompilerParams(vmem_limit_bytes=16 << 20)
    held = lambda value: pltpu.with_memory_space_constraint(value, pltpu.VMEM)
    strips = -(-len(slots(width)) // (lanes // RIGHT))

    columns = pl.pallas_call(
        table_kernel,
        out_shape=pltpu.VMEM((lanes, lanes), jnp.float32),
        out_specs=vmem,
        compiler_params=limit,
        cost_estimate=pl.CostEstimate(flops=LONG, bytes_accessed=lanes * lanes * 4, transcendentals=0),
    )()
    other = net.swap(permeability)
    up, down = net.straight(permeability, 1), net.straight(permeability, -1)
    pair, packed = pl.pallas_call(
        pack_kernel,
        out_shape=[
            pltpu.VMEM((2 * width, 3, depth, lanes), jnp.float32),
            pltpu.VMEM((2 * strips, depth, lanes), jnp.float32),
        ],
        in_specs=[vmem] * 2,
        out_specs=[vmem] * 2,
        compiler_params=limit,
    )(held(permeability), held(other))
    above, below = net.sideways(packed, 1), net.sideways(packed, -1)
    beside = net.sideways(packed, 0)
    up_other, down_other = net.swap(up), net.swap(down)
    picks = pl.pallas_call(
        picks_kernel,
        out_shape=pltpu.VMEM((8 * NCL, 8 * depth), jnp.float32),
        in_specs=[smem],
        out_specs=vmem,
        compiler_params=limit,
    )(layer_map)
    scratch = pltpu.VMEM((256, depth, lanes), jnp.float32)
    rows = LOW + 3 * width + HIGH
    stack, placed = pl.pallas_call(
        stack_kernel,
        out_shape=[pltpu.VMEM((rows, 3, depth, lanes), jnp.float32)] * 2,
        in_specs=[vmem] * 5,
        out_specs=[vmem] * 2,
        compiler_params=limit,
        cost_estimate=pl.CostEstimate(flops=LONG, bytes_accessed=4 * permeability.size * 4, transcendentals=0),
    )(held(pair), held(up), held(up_other), held(down), held(down_other))
    inner = pl.pallas_call(
        main_kernel,
        out_shape=pltpu.VMEM((8 * depth, lanes), jnp.float32),
        in_specs=[vmem] * 2,
        out_specs=vmem,
        scratch_shapes=[scratch],
        compiler_params=limit,
        cost_estimate=pl.CostEstimate(flops=LONG, bytes_accessed=4 * permeability.size * 4, transcendentals=0),
    )(held(columns), held(stack))
    joined = pl.pallas_call(
        join_kernel,
        out_shape=pltpu.VMEM((5 * strips, depth, lanes), jnp.float32),
        in_specs=[vmem] * 3,
        out_specs=vmem,
        compiler_params=limit,
    )(held(below), held(beside), held(above))
    theirs = net.swap(joined)
    out = jax.ShapeDtypeStruct((3, NCL, width // BXY, lanes // BXY), jnp.float32)
    return pl.pallas_call(
        edge_kernel,
        out_shape=(out, out),
        in_specs=[vmem] * 5,
        out_specs=(vmem, vmem),
        scratch_shapes=[scratch],
        compiler_params=limit,
    )(held(picks), held(placed), held(joined), held(theirs), held(inner))


def solution(mesh):
    in_specs = (P(None, None, "gx", "gy"), P())
    out_specs = (P(None, None, "gx", "gy"), P(None, None, "gx", "gy"))
    return jax.shard_map(local, mesh=mesh, in_specs=in_specs, out_specs=out_specs, check_vma=False)
```

```python
import functools
import math

import jax
import jax.numpy as jnp
from jax import lax
from jax.experimental import pallas as pl
from jax.experimental.pallas import tpu as pltpu
from jax.sharding import PartitionSpec as P

NCL = 4
BXY = 8
SWEEPS = 4
KMIN = 0.01
EPS = 1e-06

LOW = SWEEPS
HIGH = SWEEPS + 1
RIGHT = BXY + HIGH
FIRST, LAST = -LOW, 2 * BXY + HIGH - 1
START = RIGHT + LOW


def sweep_weights(count):
    return [
        1.0 / (1.05 + 0.95 * math.cos(math.pi * (2 * s + 1) / (2 * count))) for s in range(count)
    ]


WEIGHTS = sweep_weights(SWEEPS)


SCALES = [math.prod(WEIGHTS[: s + 1]) for s in range(SWEEPS)]


def harmonic(left, right):
    return 2.0 * left * right / (left + right)


def lanes_of(shape):
    return lax.broadcasted_iota(jnp.int32, shape, len(shape) - 1)


def up(value, axis):
    return pltpu.roll(value, value.shape[axis] - 1, axis)


def down(value, axis):
    return pltpu.roll(value, 1, axis)


def layers_of(tile, comp, row):
    _, depth, width, lanes = tile.shape
    flat = tile.reshape(3 * depth * width, lanes)
    return flat[pl.ds(comp * depth * width + row, depth, stride=width), :]


LONG = 10**10


class Solver:
    def __init__(self, inverse_of, scratch, y_ends, y_starts):
        self.inverse_of = inverse_of
        self.scratch = scratch
        self.slots = {}
        self.cache = {}
        shape = scratch.shape[1:]
        layer = lax.broadcasted_iota(jnp.int32, shape, 0)
        self.top = layer == shape[0] - 1
        self.bottom = layer == 0
        self.y_ends = y_ends
        self.y_starts = y_starts

    def memo(self, key, make):
        if key not in self.cache:
            self.cache[key] = make()
        return self.cache[key]

    def stored(self, key, make):
        if key not in self.slots:
            value = make()
            self.slots[key] = len(self.slots)
            self.scratch[self.slots[key]] = value
        return self.scratch[self.slots[key]]

    def inverse(self, comp, row):
        return self.memo(("k", comp, row), lambda: self.inverse_of(comp, row))

    def x_face(self, row):
        return self.memo(("tx", row), lambda: 1.0 / (self.inverse(0, row) + self.inverse(0, row + 1)))

    def x_edge(self, row):
        return self.memo(("te", row), lambda: 1.0 / (self.inverse(0, row) + self.inverse(0, row)))

    def y_faces(self, row):
        def make():
            here = self.inverse(1, row)
            above = up(here, 1)
            if self.y_ends is None:
                upper = 1.0 / (here + above)
                return upper, down(upper, 1)
            below = jnp.where(self.y_starts, here, down(here, 1))
            return 1.0 / (here + jnp.where(self.y_ends, here, above)), 1.0 / (here + below)

        return self.memo(("ty", row), make)

    def z_faces(self, row):
        def make():
            here = self.inverse(2, row)
            above = jnp.where(self.top, here, up(here, 0))
            below = jnp.where(self.bottom, here, down(here, 0))
            return 1.0 / (here + above), 1.0 / (here + below)

        return self.memo(("tz", row), make)

    def side_faces(self, row):
        def make():
            ty, ty_low = self.y_faces(row)
            tz, tz_low = self.z_faces(row)
            total = (ty + ty_low) + (tz + tz_low)
            if self.y_ends is not None:
                ty = jnp.where(self.y_ends, 0.0, ty)
                ty_low = jnp.where(self.y_starts, 0.0, ty_low)
            return ty, ty_low, jnp.where(self.top, 0.0, tz), jnp.where(self.bottom, 0.0, tz_low), total

        return self.memo(("side", row), make)

    def x_faces(self, row, edge):
        upper = self.x_edge(row) if edge == "up" else self.x_face(row)
        lower = self.x_edge(row) if edge == "low" else self.x_face(row - 1)
        return upper, lower

    def edge_of(self, row, boundary):
        return boundary[0] if boundary is not None and boundary[1] == row else None

    def scale(self, row, edge):
        def make():
            upper, lower = self.x_faces(row, edge)
            return 1.0 / ((upper + lower) + self.side_faces(row)[4])

        return self.memo(("h", row, edge), make)

    def weight(self, which, row, edge):
        def make():
            faces = self.x_faces(row, edge) if which < 2 else self.side_faces(row)[:4]
            return faces[which % 2 if which < 2 else which - 2] * self.scale(row, edge)

        return self.stored(("a", which, row, edge), make)

    def drive(self, d, row, edge):
        def make():
            upper, lower = (
                self.x_faces(row, edge) if d == 0 else self.y_faces(row) if d == 1 else self.z_faces(row)
            )
            return (upper - lower) * self.scale(row, edge)

        return self.stored(("c", d, row, edge), make)

    def pressure(self, d, count, row, boundary):
        if boundary is not None and abs(row - boundary[1]) >= count:
            boundary = None
        edge = self.edge_of(row, boundary)
        if count == 1:
            return self.drive(d, row, edge)

        def make():
            a = lambda which: self.weight(which, row, edge)
            here = self.pressure(d, count - 1, row, boundary)
            w = WEIGHTS[count - 1]
            if count == 2:
                total = ((1.0 - w) / w + 1.0 / SCALES[0]) * here
            else:
                total = ((1.0 - w) / w) * here + (1.0 / SCALES[count - 2]) * self.drive(d, row, edge)
            side = a(2) * up(here, 1) + a(3) * down(here, 1)
            layers = a(4) * up(here, 0) + a(5) * down(here, 0)
            if edge != "up":
                total = total + a(0) * self.pressure(d, count - 1, row + 1, boundary)
            if edge != "low":
                total = total + a(1) * self.pressure(d, count - 1, row - 1, boundary)
            return total + (side + layers)

        return self.memo(("u", d, count, row, boundary), make)

    def sums(self, d, row, boundary):
        if boundary is not None:
            reach = SWEEPS + (1 if d == 0 and boundary[0] == "up" else 0)
            if abs(row - boundary[1]) >= reach:
                boundary = None

        def make():
            here = self.pressure(d, SWEEPS, row, boundary)
            edge = self.edge_of(row, boundary)
            if d == 0:
                face = self.x_faces(row, edge)[0]
                above = None if edge == "up" else self.pressure(d, SWEEPS, row + 1, boundary)
            elif d == 1:
                face = self.y_faces(row)[0]
                above = up(here, 1)
                if self.y_ends is not None:
                    above = jnp.where(self.y_ends, 0.0, above)
            else:
                face = self.z_faces(row)[0]
                above = jnp.where(self.top, 0.0, up(here, 0))
            drop = 1.0 / SCALES[-1] - here
            if above is not None:
                drop = drop + above
            square = drop * drop
            return face * square, square

        return self.memo(("s", d, row, boundary), make)

    def block(self, d, begin, patches):
        uses = {}
        for row in range(begin, begin + BXY):
            for boundary, weight in patches:
                pair = self.sums(d, row, boundary)
                uses.setdefault(id(pair), (pair, []))[1].append(weight)
        groups = {}
        for pair, weights in uses.values():
            groups.setdefault(tuple(map(id, weights)), (weights, []))[1].append(pair)
        totals = None
        for weights, pairs in groups.values():
            part = [functools.reduce(jnp.add, parts) for parts in zip(*pairs)]
            if weights != [None]:
                factor = sum(1.0 if w is None else w for w in weights)
                part = [factor * p for p in part]
            totals = part if totals is None else [a + b for a, b in zip(totals, part)]
        return totals


def accumulate(solver, present):
    low, high, high2 = present
    own = [(("up", BXY - 1), low), (None, None), (("low", 0), high)]
    after = [(("up", 2 * BXY - 1), None), (None, None), (("low", BXY), high2)]
    jobs = [(d, 0, own) for d in range(3)] + [(0, BXY, after)]
    results = {}
    order = [jobs[0], jobs[1], jobs[2], jobs[3]]
    for row in range(BXY):
        for d, begin, patches in order:
            for boundary, _ in patches:
                solver.sums(d, begin + row, boundary)
    for i, (d, begin, patches) in enumerate(jobs):
        results[i] = solver.block(d, begin, patches)
    return [value for i in range(len(jobs)) for value in results[i]]


def thirds(value):
    parts = []
    for _ in range(3):
        parts.append(value.astype(jnp.bfloat16))
        value = value - parts[-1].astype(jnp.float32)
    return parts


def reduce_sums(sums, masks, columns):
    depth = sums[0].shape[0]
    at = lax.broadcasted_iota(jnp.int32, sums[0].shape, 0)
    per = depth // NCL
    rows = []
    for first in range(0, len(sums), per):
        value = None
        for n, total in enumerate(sums[first : first + per]):
            for layer in range(NCL):
                part = total * masks[layer]
                shift = depth // 2
                while shift:
                    part = part + pltpu.roll(part, shift, 0)
                    shift //= 2
                place_at = n * NCL + layer
                value = part if value is None else jnp.where(at < place_at, value, part)
        rows.append(value)
    value = jnp.concatenate(rows, axis=0)
    count = value.shape[0]
    parts = jnp.dot(
        jnp.concatenate(thirds(value), axis=0),
        columns,
        preferred_element_type=jnp.float32,
    )
    return parts[:count] + parts[count : 2 * count] + parts[2 * count :]


def masks_kernel(layer_map, out):
    layer = lax.broadcasted_iota(jnp.int32, out.shape[1:], 0)
    held = jnp.zeros(out.shape[1:], jnp.int32)
    for z in range(out.shape[1]):
        held = jnp.where(layer == z, layer_map[z], held)
    for coarse in range(out.shape[0]):
        out[coarse] = jnp.where(held == coarse, 1.0, 0.0)


def place(axes):
    i, j = (lax.axis_index(a) for a in axes)
    nx, ny = (lax.axis_size(a) for a in axes)
    core, chip = i % 2, i // 2
    one = lambda test: jnp.where(test, 1.0, 0.0).astype(jnp.float32)
    tiles = one(i > 0), one(i < nx - 1), one(i < nx - 2)
    chips = one(chip > 0), one(chip < nx // 2 - 1)
    return core, tiles, chips, (one(j > 0), one(j < ny - 1))


def slots(width):
    return [(comp, row) for row in range(width) for comp in range(3)]


def table_kernel(inside, edges):
    _, _, _, (has_left, has_right) = place(("gx", "gy"))
    lanes = inside.shape[0]
    count, half, start = lanes // BXY, lanes // 2, START
    r = lax.broadcasted_iota(jnp.int32, inside.shape, 0)
    c = lax.broadcasted_iota(jnp.int32, inside.shape, 1)
    inner = (r // BXY == c) & (c > 0) & (c < count - 1)
    inside[...] = jnp.where(inner, 1.0, 0.0).astype(jnp.bfloat16)

    def span(begin):
        return (r >= begin) & (r < begin + BXY)

    first = jnp.where(span(start), 1.0, 0.0) + jnp.where(span(half + start), has_left, 0.0)
    final = jnp.where(span(lanes - BXY), 1.0, 0.0) + jnp.where(span(half - BXY), has_right, 0.0)
    beyond = jnp.where(span(0) | span(half), has_right, 0.0)
    columns = jnp.where(
        c == 0, first, jnp.where(c == count - 1, final, jnp.where(c == count, beyond, 0.0))
    )
    edges[...] = columns.astype(jnp.bfloat16)


def pack_kernel(mine, other, pair, packed):
    core, _, _, _ = place(("gx", "gy"))
    _, depth, width, lanes = mine.shape
    per = lanes // RIGHT
    lane = lanes_of((depth, lanes))
    rows = slots(width)
    count = packed.shape[0] // 2
    for tile, at in ((mine, core), (other, 1 - core)):
        strip = None
        for n, (comp, row) in enumerate(rows):
            value = layers_of(tile, comp, row)
            pair[at * width + row, comp] = value
            shift = RIGHT * (n % per)
            value = pltpu.roll(value, shift + core * START, 1)
            strip = value if n % per == 0 else jnp.where(lane < shift + core * RIGHT, strip, value)
            if n % per == per - 1 or n == len(rows) - 1:
                packed[at * count + n // per] = strip


def join_kernel(below, beside, above, out):
    core, _, (has_down, has_up), (has_left, has_right) = place(("gx", "gy"))
    side = jnp.where(core == 0, has_right, has_left)
    half = beside.shape[0] // 2
    out[:half] = 1.0 / (below[half:] * (side * has_down) + KMIN)
    out[half : 3 * half] = 1.0 / (beside[...] * side + KMIN)
    out[3 * half :] = 1.0 / (above[...] * (side * has_up) + KMIN)


def needed():
    return [(row, comp) for row in range(FIRST, LAST + 1) for comp in range(1 if row in (FIRST, LAST) else 3)]


def with_strips(core, strips, of, width, shape):
    lanes = shape[-1]
    lane = lanes_of(shape)
    begin, end = of * RIGHT, RIGHT + of * LOW
    near = (lane >= begin) & (lane < end)
    far = (lane >= lanes // 2 + begin) & (lane < lanes // 2 + end)
    per, per_tile = lanes // RIGHT, strips.shape[0] // 5
    index = {key: at for at, key in enumerate(slots(width))}

    def put(row, comp, value):
        at = index[comp, row % width]
        strip = strips[(core + 1 + row // width) * per_tile + at // per]
        shift = -RIGHT * (at % per) % lanes
        value = jnp.where(far, pltpu.roll(strip, (shift + lanes // 2) % lanes, 1), value)
        return jnp.where(near, pltpu.roll(strip, shift, 1) if shift else strip, value)

    return put


def stack_kernel(pair, up_mine, up_other, down_mine, down_other, stack, placed):
    core, _, (has_down, has_up), _ = place(("gx", "gy"))
    width = up_mine.shape[2]
    depth, lanes = pair.shape[2:]
    first = core == 0
    lane = lanes_of((depth, lanes))
    half, start = lanes // 2, START
    stop = start + BXY + HIGH
    near = (lane >= start) & (lane < stop)
    second = (lane >= half - BXY - LOW) & (lane < half + stop)

    def put(row, comp, value):
        value = 1.0 / (value + KMIN)
        stack[LOW + row, comp] = value
        value = jnp.where(near, pltpu.roll(value, start, 1), value)
        placed[LOW + row, comp] = jnp.where(second, pltpu.roll(value, half, 1), value)

    for row in range(2 * width):
        for comp in range(3):
            put(row, comp, pair[row, comp])
    for row in range(width):
        for comp in range(3):
            mine, other = layers_of(up_mine, comp, row), layers_of(up_other, comp, row)
            put(2 * width + row, comp, jnp.where(first, mine, other) * has_up)
            if row < HIGH:
                put(3 * width + row, comp, jnp.where(first, other, mine) * has_up)
            if row >= width - LOW:
                mine, other = layers_of(down_mine, comp, row), layers_of(down_other, comp, row)
                put(row - width, comp, jnp.where(first, other, mine) * has_down)


def main_kernel(columns, masks, stack, placed, mine, out, rows, scratch):
    core, present, _, _ = place(("gx", "gy"))
    base = LOW + core * BXY
    solver = Solver(lambda comp, row: stack[base + row, comp], scratch, None, None)
    out[...] = reduce_sums(accumulate(solver, present), masks, columns[...])
    put = with_strips(core, mine, core, BXY, placed.shape[2:])
    for row, comp in needed():
        rows[row - FIRST, comp] = put(row, comp, placed[base + row, comp])


def edge_kernel(columns, masks, rows, other, inner, perm_out, trans_out, scratch):
    core, present, _, _ = place(("gx", "gy"))
    depth, lanes = rows.shape[2:]
    width = BXY
    lane = lanes_of((depth, lanes))
    half, start = lanes // 2, START
    put = with_strips(core, other, 1 - core, width, (depth, lanes))

    def inverse(comp, row):
        return put(row, comp, rows[row - FIRST, comp])

    y_ends = (lane == BXY - 1) | (lane == half + start + BXY - 1)
    y_starts = lane == half - BXY
    solver = Solver(inverse, scratch, y_ends, y_starts)
    sums = accumulate(solver, present)
    count = lanes // BXY
    total = inner[...] + reduce_sums(sums, masks, columns[...])
    cells = (width + 2 * BXY, lanes + 2 * BXY, depth)
    energy = [total[2 * NCL * q : 2 * NCL * q + NCL] for q in range(4)]
    square = [total[2 * NCL * q + NCL : 2 * NCL * (q + 1)] for q in range(4)]
    perms = [
        2.0 * energy[q] / (square[q] + EPS * (cells[d] / SCALES[-1]) ** 2)
        for q, d in enumerate((0, 1, 2, 0))
    ]
    layer = lax.broadcasted_iota(jnp.int32, perms[0].shape, 0)
    trans = [
        harmonic(perms[0], perms[3] * present[1]),
        harmonic(perms[1], up(perms[1], 1)),
    ]
    above = jnp.concatenate([perms[2][1:], jnp.zeros_like(perms[2][:1])], axis=0)
    trans.append(harmonic(perms[2], above))
    for d in range(3):
        for l in range(NCL):
            perm_out[d, l, :, :] = perms[d][l : l + 1, :count]
            trans_out[d, l, :, :] = trans[d][l : l + 1, :count]


class Exchange:
    def __init__(self, axes):
        self.axes = axes
        self.nx, self.ny = (lax.axis_size(a) for a in axes)
        self.sent = {}

    def permute(self, value, target):
        nx, ny = self.nx, self.ny
        pairs = []
        for i in range(nx):
            for j in range(ny):
                a, b = target(i, j)
                pairs.append((i * ny + j, a % nx * ny + b))
        key = (id(value), tuple(pairs))
        if key not in self.sent:
            self.sent[key] = (value, lax.ppermute(value, self.axes, pairs))
        return self.sent[key][1]

    def swap(self, value):
        return self.permute(value, lambda i, j: (i ^ 1, j))

    def straight(self, value, pairs):
        return self.permute(value, lambda i, j: (i - 2 * pairs, j))

    def sideways(self, value, pairs):
        def target(i, j):
            to = j - 1 if i % 2 == 0 else j + 1
            i -= 2 * pairs
            return (i, to) if 0 <= to < self.ny else (i ^ 1, j)

        return self.permute(value, target)


def local(permeability, layer_map):
    _, depth, width, lanes = permeability.shape
    net = Exchange(("gx", "gy"))
    if width != BXY or depth != 8 or lanes != 128 or net.nx % 2:
        raise ValueError("unsupported tile")
    vmem = pl.BlockSpec(memory_space=pltpu.VMEM)
    smem = pl.BlockSpec(memory_space=pltpu.SMEM)
    limit = pltpu.CompilerParams(vmem_limit_bytes=16 << 20)
    held = lambda value: pltpu.with_memory_space_constraint(value, pltpu.VMEM)
    strips = -(-len(slots(width)) // (lanes // RIGHT))

    inside, edges = pl.pallas_call(
        table_kernel,
        out_shape=[pltpu.VMEM((lanes, lanes), jnp.bfloat16)] * 2,
        out_specs=[vmem] * 2,
        compiler_params=limit,
        cost_estimate=pl.CostEstimate(flops=LONG, bytes_accessed=lanes * lanes * 4, transcendentals=0),
    )()
    other = net.swap(permeability)
    up, down = net.straight(permeability, 1), net.straight(permeability, -1)
    pair, packed = pl.pallas_call(
        pack_kernel,
        out_shape=[
            pltpu.VMEM((2 * width, 3, depth, lanes), jnp.float32),
            pltpu.VMEM((2 * strips, depth, lanes), jnp.float32),
        ],
        in_specs=[vmem] * 2,
        out_specs=[vmem] * 2,
        compiler_params=limit,
    )(held(permeability), held(other))
    above, below = net.sideways(packed, 1), net.sideways(packed, -1)
    beside = net.sideways(packed, 0)
    up_other, down_other = net.swap(up), net.swap(down)
    masks = pl.pallas_call(
        masks_kernel,
        out_shape=pltpu.VMEM((NCL, depth, lanes), jnp.float32),
        in_specs=[smem],
        out_specs=vmem,
        compiler_params=limit,
    )(layer_map)
    scratch = pltpu.VMEM((256, depth, lanes), jnp.float32)
    rows = LOW + 3 * width + HIGH
    stack, placed = pl.pallas_call(
        stack_kernel,
        out_shape=[pltpu.VMEM((rows, 3, depth, lanes), jnp.float32)] * 2,
        in_specs=[vmem] * 5,
        out_specs=[vmem] * 2,
        compiler_params=limit,
        cost_estimate=pl.CostEstimate(flops=LONG, bytes_accessed=4 * permeability.size * 4, transcendentals=0),
    )(held(pair), held(up), held(up_other), held(down), held(down_other))
    joined = pl.pallas_call(
        join_kernel,
        out_shape=pltpu.VMEM((5 * strips, depth, lanes), jnp.float32),
        in_specs=[vmem] * 3,
        out_specs=vmem,
        compiler_params=limit,
    )(held(below), held(beside), held(above))
    theirs = net.swap(joined)
    inner, near = pl.pallas_call(
        main_kernel,
        out_shape=[
            pltpu.VMEM((8 * NCL, lanes), jnp.float32),
            pltpu.VMEM((LAST + 1 - FIRST, 3, depth, lanes), jnp.float32),
        ],
        in_specs=[vmem] * 5,
        out_specs=[vmem] * 2,
        scratch_shapes=[scratch],
        compiler_params=limit,
        cost_estimate=pl.CostEstimate(flops=LONG, bytes_accessed=4 * permeability.size * 4, transcendentals=0),
    )(held(inside), held(masks), held(stack), held(placed), held(joined))
    out = jax.ShapeDtypeStruct((3, NCL, width // BXY, lanes // BXY), jnp.float32)
    return pl.pallas_call(
        edge_kernel,
        out_shape=(out, out),
        in_specs=[vmem] * 5,
        out_specs=(vmem, vmem),
        scratch_shapes=[scratch],
        compiler_params=limit,
    )(held(edges), held(masks), held(near), held(theirs), held(inner))


def solution(mesh):
    in_specs = (P(None, None, "gx", "gy"), P())
    out_specs = (P(None, None, "gx", "gy"), P(None, None, "gx", "gy"))
    return jax.shard_map(local, mesh=mesh, in_specs=in_specs, out_specs=out_specs, check_vma=False)
```

```python
import functools
import math

import jax
import jax.numpy as jnp
from jax import lax
from jax.experimental import pallas as pl
from jax.experimental.pallas import tpu as pltpu
from jax.sharding import PartitionSpec as P

NCL = 4
BXY = 8
SWEEPS = 4
KMIN = 0.01
EPS = 1e-06

LOW = SWEEPS
HIGH = SWEEPS + 1
RIGHT = BXY + HIGH
FIRST, LAST = -LOW, 2 * BXY + HIGH - 1
START = RIGHT + LOW


def sweep_weights(count):
    return [
        1.0 / (1.05 + 0.95 * math.cos(math.pi * (2 * s + 1) / (2 * count))) for s in range(count)
    ]


WEIGHTS = sweep_weights(SWEEPS)


def sweep_polynomial(weights):
    left = [1.0]
    for w in weights:
        grown = [0.0] * (len(left) + 1)
        for i, value in enumerate(left):
            grown[i] += (1.0 - w) * value
            grown[i + 1] += w * value
        left = grown
    total, out = 1.0, []
    for value in left[:-1]:
        total -= value
        out.append(total)
    return out


POLYNOMIAL = sweep_polynomial(WEIGHTS)


def harmonic(left, right):
    return 2.0 * left * right / (left + right)


def lanes_of(shape):
    return lax.broadcasted_iota(jnp.int32, shape, len(shape) - 1)


def up(value, axis):
    return pltpu.roll(value, value.shape[axis] - 1, axis)


def down(value, axis):
    return pltpu.roll(value, 1, axis)


def layers_of(tile, comp, row):
    _, depth, width, lanes = tile.shape
    flat = tile.reshape(3 * depth * width, lanes)
    return flat[pl.ds(comp * depth * width + row, depth, stride=width), :]


LONG = 10**10


class Solver:
    def __init__(self, inverse_of, scratch, y_ends, y_starts):
        self.inverse_of = inverse_of
        self.scratch = scratch
        self.slots = {}
        self.cache = {}
        shape = scratch.shape[1:]
        layer = lax.broadcasted_iota(jnp.int32, shape, 0)
        self.top = layer == shape[0] - 1
        self.bottom = layer == 0
        self.y_ends = y_ends
        self.y_starts = y_starts

    def memo(self, key, make):
        if key not in self.cache:
            self.cache[key] = make()
        return self.cache[key]

    def stored(self, key, make):
        if key not in self.slots:
            value = make()
            self.slots[key] = len(self.slots)
            self.scratch[self.slots[key]] = value
        return self.scratch[self.slots[key]]

    def inverse(self, comp, row):
        return self.memo(("k", comp, row), lambda: self.inverse_of(comp, row))

    def x_face(self, row):
        return self.memo(("tx", row), lambda: 1.0 / (self.inverse(0, row) + self.inverse(0, row + 1)))

    def x_edge(self, row):
        return self.memo(("te", row), lambda: 1.0 / (self.inverse(0, row) + self.inverse(0, row)))

    def y_faces(self, row):
        def make():
            here = self.inverse(1, row)
            above = up(here, 1)
            if self.y_ends is None:
                upper = 1.0 / (here + above)
                return upper, down(upper, 1)
            below = jnp.where(self.y_starts, here, down(here, 1))
            return 1.0 / (here + jnp.where(self.y_ends, here, above)), 1.0 / (here + below)

        return self.memo(("ty", row), make)

    def z_faces(self, row):
        def make():
            here = self.inverse(2, row)
            above = jnp.where(self.top, here, up(here, 0))
            below = jnp.where(self.bottom, here, down(here, 0))
            return 1.0 / (here + above), 1.0 / (here + below)

        return self.memo(("tz", row), make)

    def side_faces(self, row):
        def make():
            ty, ty_low = self.y_faces(row)
            tz, tz_low = self.z_faces(row)
            total = (ty + ty_low) + (tz + tz_low)
            if self.y_ends is not None:
                ty = jnp.where(self.y_ends, 0.0, ty)
                ty_low = jnp.where(self.y_starts, 0.0, ty_low)
            return ty, ty_low, jnp.where(self.top, 0.0, tz), jnp.where(self.bottom, 0.0, tz_low), total

        return self.memo(("side", row), make)

    def x_faces(self, row, edge):
        upper = self.x_edge(row) if edge == "up" else self.x_face(row)
        lower = self.x_edge(row) if edge == "low" else self.x_face(row - 1)
        return upper, lower

    def edge_of(self, row, boundary):
        return boundary[0] if boundary is not None and boundary[1] == row else None

    def scale(self, row, edge):
        def make():
            upper, lower = self.x_faces(row, edge)
            return 1.0 / ((upper + lower) + self.side_faces(row)[4])

        return self.memo(("h", row, edge), make)

    def weight(self, which, row, edge):
        def make():
            faces = self.x_faces(row, edge) if which < 2 else self.side_faces(row)[:4]
            return faces[which % 2 if which < 2 else which - 2] * self.scale(row, edge)

        return self.stored(("a", which, row, edge), make)

    def drive(self, d, row, edge):
        def make():
            upper, lower = (
                self.x_faces(row, edge) if d == 0 else self.y_faces(row) if d == 1 else self.z_faces(row)
            )
            return (upper - lower) * self.scale(row, edge)

        return self.stored(("c", d, row, edge), make)

    def pressure(self, d, count, row, boundary):
        if boundary is not None and abs(row - boundary[1]) >= count:
            boundary = None
        edge = self.edge_of(row, boundary)
        if count == 1:
            return self.drive(d, row, edge)

        def make():
            a = lambda which: self.weight(which, row, edge)
            here = self.pressure(d, count - 1, row, boundary)
            total = (POLYNOMIAL[SWEEPS - count] / POLYNOMIAL[-1]) * self.drive(d, row, edge)
            side = a(2) * up(here, 1) + a(3) * down(here, 1)
            layers = a(4) * up(here, 0) + a(5) * down(here, 0)
            if edge != "up":
                total = total + a(0) * self.pressure(d, count - 1, row + 1, boundary)
            if edge != "low":
                total = total + a(1) * self.pressure(d, count - 1, row - 1, boundary)
            return total + (side + layers)

        return self.memo(("u", d, count, row, boundary), make)

    def sums(self, d, row, boundary):
        if boundary is not None:
            reach = SWEEPS + (1 if d == 0 and boundary[0] == "up" else 0)
            if abs(row - boundary[1]) >= reach:
                boundary = None

        def make():
            here = self.pressure(d, SWEEPS, row, boundary)
            edge = self.edge_of(row, boundary)
            if d == 0:
                face = self.x_faces(row, edge)[0]
                above = None if edge == "up" else self.pressure(d, SWEEPS, row + 1, boundary)
            elif d == 1:
                face = self.y_faces(row)[0]
                above = up(here, 1)
                if self.y_ends is not None:
                    above = jnp.where(self.y_ends, 0.0, above)
            else:
                face = self.z_faces(row)[0]
                above = jnp.where(self.top, 0.0, up(here, 0))
            drop = 1.0 / POLYNOMIAL[-1] - here
            if above is not None:
                drop = drop + above
            square = drop * drop
            return face * square, square

        return self.memo(("s", d, row, boundary), make)

    def block(self, d, begin, patches):
        uses = {}
        for row in range(begin, begin + BXY):
            for boundary, weight in patches:
                pair = self.sums(d, row, boundary)
                uses.setdefault(id(pair), (pair, []))[1].append(weight)
        groups = {}
        for pair, weights in uses.values():
            groups.setdefault(tuple(map(id, weights)), (weights, []))[1].append(pair)
        totals = None
        for weights, pairs in groups.values():
            part = [functools.reduce(jnp.add, parts) for parts in zip(*pairs)]
            if weights != [None]:
                factor = sum(1.0 if w is None else w for w in weights)
                part = [factor * p for p in part]
            totals = part if totals is None else [a + b for a, b in zip(totals, part)]
        return totals


def accumulate(solver, present):
    low, high, high2 = present
    own = [(("up", BXY - 1), low), (None, None), (("low", 0), high)]
    after = [(("up", 2 * BXY - 1), None), (None, None), (("low", BXY), high2)]
    jobs = [(d, 0, own) for d in range(3)] + [(0, BXY, after)]
    results = {}
    order = [jobs[1], jobs[2], jobs[0], jobs[3]]
    for row in range(BXY):
        for d, begin, patches in order:
            for boundary, _ in patches:
                solver.sums(d, begin + row, boundary)
    for i, (d, begin, patches) in enumerate(jobs):
        results[i] = solver.block(d, begin, patches)
    return [value for i in range(len(jobs)) for value in results[i]]


def thirds(value):
    parts = []
    for _ in range(3):
        parts.append(value.astype(jnp.bfloat16))
        value = value - parts[-1].astype(jnp.float32)
    return parts


def reduce_sums(sums, masks, columns):
    depth = sums[0].shape[0]
    at = lax.broadcasted_iota(jnp.int32, sums[0].shape, 0)
    per = depth // NCL
    rows = []
    for first in range(0, len(sums), per):
        value = None
        for n, total in enumerate(sums[first : first + per]):
            for layer in range(NCL):
                part = total * masks[layer]
                shift = depth // 2
                while shift:
                    part = part + pltpu.roll(part, shift, 0)
                    shift //= 2
                place_at = n * NCL + layer
                value = part if value is None else jnp.where(at < place_at, value, part)
        rows.append(value)
    value = jnp.concatenate(rows, axis=0)
    count = value.shape[0]
    parts = jnp.dot(
        jnp.concatenate(thirds(value), axis=0),
        columns,
        preferred_element_type=jnp.float32,
    )
    return parts[:count] + parts[count : 2 * count] + parts[2 * count :]


def masks_kernel(layer_map, out):
    layer = lax.broadcasted_iota(jnp.int32, out.shape[1:], 0)
    held = jnp.zeros(out.shape[1:], jnp.int32)
    for z in range(out.shape[1]):
        held = jnp.where(layer == z, layer_map[z], held)
    for coarse in range(out.shape[0]):
        out[coarse] = jnp.where(held == coarse, 1.0, 0.0)


def place(axes):
    i, j = (lax.axis_index(a) for a in axes)
    nx, ny = (lax.axis_size(a) for a in axes)
    core, chip = i % 2, i // 2
    one = lambda test: jnp.where(test, 1.0, 0.0).astype(jnp.float32)
    tiles = one(i > 0), one(i < nx - 1), one(i < nx - 2)
    chips = one(chip > 0), one(chip < nx // 2 - 1)
    return core, tiles, chips, (one(j > 0), one(j < ny - 1))


def slots(width):
    return [(comp, row) for row in range(width) for comp in range(3)]


def table_kernel(inside, edges):
    _, _, _, (has_left, has_right) = place(("gx", "gy"))
    lanes = inside.shape[0]
    count, half, start = lanes // BXY, lanes // 2, START
    r = lax.broadcasted_iota(jnp.int32, inside.shape, 0)
    c = lax.broadcasted_iota(jnp.int32, inside.shape, 1)
    inner = (r // BXY == c) & (c > 0) & (c < count - 1)
    inside[...] = jnp.where(inner, 1.0, 0.0).astype(jnp.bfloat16)

    def span(begin):
        return (r >= begin) & (r < begin + BXY)

    first = jnp.where(span(start), 1.0, 0.0) + jnp.where(span(half + start), has_left, 0.0)
    final = jnp.where(span(lanes - BXY), 1.0, 0.0) + jnp.where(span(half - BXY), has_right, 0.0)
    beyond = jnp.where(span(0) | span(half), has_right, 0.0)
    columns = jnp.where(
        c == 0, first, jnp.where(c == count - 1, final, jnp.where(c == count, beyond, 0.0))
    )
    edges[...] = columns.astype(jnp.bfloat16)


def pack_kernel(mine, other, pair, packed):
    core, _, _, _ = place(("gx", "gy"))
    _, depth, width, lanes = mine.shape
    per = lanes // RIGHT
    lane = lanes_of((depth, lanes))
    rows = slots(width)
    count = packed.shape[0] // 2
    for tile, at in ((mine, core), (other, 1 - core)):
        strip = None
        for n, (comp, row) in enumerate(rows):
            value = layers_of(tile, comp, row)
            pair[at * width + row, comp] = value
            shift = RIGHT * (n % per)
            value = pltpu.roll(value, shift + core * START, 1)
            strip = value if n % per == 0 else jnp.where(lane < shift + core * RIGHT, strip, value)
            if n % per == per - 1 or n == len(rows) - 1:
                packed[at * count + n // per] = strip


def join_kernel(below, beside, above, out):
    core, _, (has_down, has_up), (has_left, has_right) = place(("gx", "gy"))
    side = jnp.where(core == 0, has_right, has_left)
    half = beside.shape[0] // 2
    out[:half] = 1.0 / (below[half:] * (side * has_down) + KMIN)
    out[half : 3 * half] = 1.0 / (beside[...] * side + KMIN)
    out[3 * half :] = 1.0 / (above[...] * (side * has_up) + KMIN)


def needed():
    return [(row, comp) for row in range(FIRST, LAST + 1) for comp in range(1 if row in (FIRST, LAST) else 3)]


def with_strips(core, strips, of, width, shape):
    lanes = shape[-1]
    lane = lanes_of(shape)
    begin, end = of * RIGHT, RIGHT + of * LOW
    near = (lane >= begin) & (lane < end)
    far = (lane >= lanes // 2 + begin) & (lane < lanes // 2 + end)
    per, per_tile = lanes // RIGHT, strips.shape[0] // 5
    index = {key: at for at, key in enumerate(slots(width))}

    def put(row, comp, value):
        at = index[comp, row % width]
        strip = strips[(core + 1 + row // width) * per_tile + at // per]
        shift = -RIGHT * (at % per) % lanes
        value = jnp.where(far, pltpu.roll(strip, (shift + lanes // 2) % lanes, 1), value)
        return jnp.where(near, pltpu.roll(strip, shift, 1) if shift else strip, value)

    return put


def stack_kernel(pair, up_mine, up_other, down_mine, down_other, stack, placed):
    core, _, (has_down, has_up), _ = place(("gx", "gy"))
    width = up_mine.shape[2]
    depth, lanes = pair.shape[2:]
    first = core == 0
    lane = lanes_of((depth, lanes))
    half, start = lanes // 2, START
    stop = start + BXY + HIGH
    near = (lane >= start) & (lane < stop)
    second = (lane >= half - BXY - LOW) & (lane < half + stop)

    def put(row, comp, value):
        value = 1.0 / (value + KMIN)
        stack[LOW + row, comp] = value
        value = jnp.where(near, pltpu.roll(value, start, 1), value)
        placed[LOW + row, comp] = jnp.where(second, pltpu.roll(value, half, 1), value)

    for row in range(2 * width):
        for comp in range(3):
            put(row, comp, pair[row, comp])
    for row in range(width):
        for comp in range(3):
            mine, other = layers_of(up_mine, comp, row), layers_of(up_other, comp, row)
            put(2 * width + row, comp, jnp.where(first, mine, other) * has_up)
            if row < HIGH:
                put(3 * width + row, comp, jnp.where(first, other, mine) * has_up)
            if row >= width - LOW:
                mine, other = layers_of(down_mine, comp, row), layers_of(down_other, comp, row)
                put(row - width, comp, jnp.where(first, other, mine) * has_down)


def main_kernel(columns, masks, stack, placed, mine, out, rows, scratch):
    core, present, _, _ = place(("gx", "gy"))
    base = LOW + core * BXY
    solver = Solver(lambda comp, row: stack[base + row, comp], scratch, None, None)
    out[...] = reduce_sums(accumulate(solver, present), masks, columns[...])
    put = with_strips(core, mine, core, BXY, placed.shape[2:])
    for row, comp in needed():
        rows[row - FIRST, comp] = put(row, comp, placed[base + row, comp])


def edge_kernel(columns, masks, rows, other, inner, perm_out, trans_out, scratch):
    core, present, _, _ = place(("gx", "gy"))
    depth, lanes = rows.shape[2:]
    width = BXY
    lane = lanes_of((depth, lanes))
    half, start = lanes // 2, START
    put = with_strips(core, other, 1 - core, width, (depth, lanes))

    def inverse(comp, row):
        return put(row, comp, rows[row - FIRST, comp])

    y_ends = (lane == BXY - 1) | (lane == half + start + BXY - 1)
    y_starts = lane == half - BXY
    solver = Solver(inverse, scratch, y_ends, y_starts)
    sums = accumulate(solver, present)
    count = lanes // BXY
    total = inner[...] + reduce_sums(sums, masks, columns[...])
    cells = (width + 2 * BXY, lanes + 2 * BXY, depth)
    energy = [total[2 * NCL * q : 2 * NCL * q + NCL] for q in range(4)]
    square = [total[2 * NCL * q + NCL : 2 * NCL * (q + 1)] for q in range(4)]
    perms = [
        2.0 * energy[q] / (square[q] + EPS * (cells[d] / POLYNOMIAL[-1]) ** 2)
        for q, d in enumerate((0, 1, 2, 0))
    ]
    layer = lax.broadcasted_iota(jnp.int32, perms[0].shape, 0)
    trans = [
        harmonic(perms[0], perms[3] * present[1]),
        harmonic(perms[1], up(perms[1], 1)),
    ]
    above = jnp.concatenate([perms[2][1:], jnp.zeros_like(perms[2][:1])], axis=0)
    trans.append(harmonic(perms[2], above))
    for d in range(3):
        for l in range(NCL):
            perm_out[d, l, :, :] = perms[d][l : l + 1, :count]
            trans_out[d, l, :, :] = trans[d][l : l + 1, :count]


class Exchange:
    def __init__(self, axes):
        self.axes = axes
        self.nx, self.ny = (lax.axis_size(a) for a in axes)
        self.sent = {}

    def permute(self, value, target):
        nx, ny = self.nx, self.ny
        pairs = []
        for i in range(nx):
            for j in range(ny):
                a, b = target(i, j)
                pairs.append((i * ny + j, a % nx * ny + b))
        key = (id(value), tuple(pairs))
        if key not in self.sent:
            self.sent[key] = (value, lax.ppermute(value, self.axes, pairs))
        return self.sent[key][1]

    def swap(self, value):
        return self.permute(value, lambda i, j: (i ^ 1, j))

    def straight(self, value, pairs):
        return self.permute(value, lambda i, j: (i - 2 * pairs, j))

    def sideways(self, value, pairs):
        def target(i, j):
            to = j - 1 if i % 2 == 0 else j + 1
            i -= 2 * pairs
            return (i, to) if 0 <= to < self.ny else (i ^ 1, j)

        return self.permute(value, target)


def local(permeability, layer_map):
    _, depth, width, lanes = permeability.shape
    net = Exchange(("gx", "gy"))
    if width != BXY or depth != 8 or lanes != 128 or net.nx % 2:
        raise ValueError("unsupported tile")
    vmem = pl.BlockSpec(memory_space=pltpu.VMEM)
    smem = pl.BlockSpec(memory_space=pltpu.SMEM)
    limit = pltpu.CompilerParams(vmem_limit_bytes=16 << 20)
    held = lambda value: pltpu.with_memory_space_constraint(value, pltpu.VMEM)
    strips = -(-len(slots(width)) // (lanes // RIGHT))

    inside, edges = pl.pallas_call(
        table_kernel,
        out_shape=[pltpu.VMEM((lanes, lanes), jnp.bfloat16)] * 2,
        out_specs=[vmem] * 2,
        compiler_params=limit,
        cost_estimate=pl.CostEstimate(flops=LONG, bytes_accessed=lanes * lanes * 4, transcendentals=0),
    )()
    other = net.swap(permeability)
    up, down = net.straight(permeability, 1), net.straight(permeability, -1)
    pair, packed = pl.pallas_call(
        pack_kernel,
        out_shape=[
            pltpu.VMEM((2 * width, 3, depth, lanes), jnp.float32),
            pltpu.VMEM((2 * strips, depth, lanes), jnp.float32),
        ],
        in_specs=[vmem] * 2,
        out_specs=[vmem] * 2,
        compiler_params=limit,
    )(held(permeability), held(other))
    above, below = net.sideways(packed, 1), net.sideways(packed, -1)
    beside = net.sideways(packed, 0)
    up_other, down_other = net.swap(up), net.swap(down)
    masks = pl.pallas_call(
        masks_kernel,
        out_shape=pltpu.VMEM((NCL, depth, lanes), jnp.float32),
        in_specs=[smem],
        out_specs=vmem,
        compiler_params=limit,
    )(layer_map)
    scratch = pltpu.VMEM((256, depth, lanes), jnp.float32)
    rows = LOW + 3 * width + HIGH
    stack, placed = pl.pallas_call(
        stack_kernel,
        out_shape=[pltpu.VMEM((rows, 3, depth, lanes), jnp.float32)] * 2,
        in_specs=[vmem] * 5,
        out_specs=[vmem] * 2,
        compiler_params=limit,
        cost_estimate=pl.CostEstimate(flops=LONG, bytes_accessed=4 * permeability.size * 4, transcendentals=0),
    )(held(pair), held(up), held(up_other), held(down), held(down_other))
    joined = pl.pallas_call(
        join_kernel,
        out_shape=pltpu.VMEM((5 * strips, depth, lanes), jnp.float32),
        in_specs=[vmem] * 3,
        out_specs=vmem,
        compiler_params=limit,
    )(held(below), held(beside), held(above))
    theirs = net.swap(joined)
    inner, near = pl.pallas_call(
        main_kernel,
        out_shape=[
            pltpu.VMEM((8 * NCL, lanes), jnp.float32),
            pltpu.VMEM((LAST + 1 - FIRST, 3, depth, lanes), jnp.float32),
        ],
        in_specs=[vmem] * 5,
        out_specs=[vmem] * 2,
        scratch_shapes=[scratch],
        compiler_params=limit,
        cost_estimate=pl.CostEstimate(flops=LONG, bytes_accessed=4 * permeability.size * 4, transcendentals=0),
    )(held(inside), held(masks), held(stack), held(placed), held(joined))
    out = jax.ShapeDtypeStruct((3, NCL, width // BXY, lanes // BXY), jnp.float32)
    return pl.pallas_call(
        edge_kernel,
        out_shape=(out, out),
        in_specs=[vmem] * 5,
        out_specs=(vmem, vmem),
        scratch_shapes=[scratch],
        compiler_params=limit,
    )(held(edges), held(masks), held(near), held(theirs), held(inner))


def solution(mesh):
    in_specs = (P(None, None, "gx", "gy"), P())
    out_specs = (P(None, None, "gx", "gy"), P(None, None, "gx", "gy"))
    return jax.shard_map(local, mesh=mesh, in_specs=in_specs, out_specs=out_specs, check_vma=False)
```

```python
import functools
import math

import jax
import jax.numpy as jnp
from jax import lax
from jax.experimental import pallas as pl
from jax.experimental.pallas import tpu as pltpu
from jax.sharding import PartitionSpec as P

NCL = 4
BXY = 8
SWEEPS = 4
KMIN = 0.01
EPS = 1e-06

LOW = SWEEPS
HIGH = SWEEPS + 1
RIGHT = BXY + HIGH
FIRST, LAST = -LOW, 2 * BXY + HIGH - 1
START = RIGHT + LOW


def sweep_weights(count):
    return [
        1.0 / (1.05 + 0.95 * math.cos(math.pi * (2 * s + 1) / (2 * count))) for s in range(count)
    ]


WEIGHTS = sweep_weights(SWEEPS)


def sweep_polynomial(weights):
    left = [1.0]
    for w in weights:
        grown = [0.0] * (len(left) + 1)
        for i, value in enumerate(left):
            grown[i] += (1.0 - w) * value
            grown[i + 1] += w * value
        left = grown
    total, out = 1.0, []
    for value in left[:-1]:
        total -= value
        out.append(total)
    return out


POLYNOMIAL = sweep_polynomial(WEIGHTS)


def harmonic(left, right):
    return 2.0 * left * right / (left + right)


def lanes_of(shape):
    return lax.broadcasted_iota(jnp.int32, shape, len(shape) - 1)


def up(value, axis):
    return pltpu.roll(value, value.shape[axis] - 1, axis)


def down(value, axis):
    return pltpu.roll(value, 1, axis)


def layers_of(tile, comp, row):
    _, depth, width, lanes = tile.shape
    flat = tile.reshape(3 * depth * width, lanes)
    return flat[pl.ds(comp * depth * width + row, depth, stride=width), :]


LONG = 10**10


class Solver:
    def __init__(self, inverse_of, scratch, y_ends, y_starts):
        self.inverse_of = inverse_of
        self.scratch = scratch
        self.slots = {}
        self.cache = {}
        shape = scratch.shape[1:]
        layer = lax.broadcasted_iota(jnp.int32, shape, 0)
        self.top = layer == shape[0] - 1
        self.bottom = layer == 0
        self.y_ends = y_ends
        self.y_starts = y_starts

    def memo(self, key, make):
        if key not in self.cache:
            self.cache[key] = make()
        return self.cache[key]

    def stored(self, key, make):
        if key not in self.slots:
            value = make()
            self.slots[key] = len(self.slots)
            self.scratch[self.slots[key]] = value
        return self.scratch[self.slots[key]]

    def inverse(self, comp, row):
        return self.memo(("k", comp, row), lambda: self.inverse_of(comp, row))

    def x_face(self, row):
        return self.memo(("tx", row), lambda: 1.0 / (self.inverse(0, row) + self.inverse(0, row + 1)))

    def x_edge(self, row):
        return self.memo(("te", row), lambda: 1.0 / (self.inverse(0, row) + self.inverse(0, row)))

    def y_faces(self, row):
        def make():
            here = self.inverse(1, row)
            above = up(here, 1)
            if self.y_ends is None:
                upper = 1.0 / (here + above)
                return upper, down(upper, 1)
            below = jnp.where(self.y_starts, here, down(here, 1))
            return 1.0 / (here + jnp.where(self.y_ends, here, above)), 1.0 / (here + below)

        return self.memo(("ty", row), make)

    def z_faces(self, row):
        def make():
            here = self.inverse(2, row)
            above = jnp.where(self.top, here, up(here, 0))
            below = jnp.where(self.bottom, here, down(here, 0))
            return 1.0 / (here + above), 1.0 / (here + below)

        return self.memo(("tz", row), make)

    def side_faces(self, row):
        def make():
            ty, ty_low = self.y_faces(row)
            tz, tz_low = self.z_faces(row)
            total = (ty + ty_low) + (tz + tz_low)
            if self.y_ends is not None:
                ty = jnp.where(self.y_ends, 0.0, ty)
                ty_low = jnp.where(self.y_starts, 0.0, ty_low)
            return ty, ty_low, jnp.where(self.top, 0.0, tz), jnp.where(self.bottom, 0.0, tz_low), total

        return self.memo(("side", row), make)

    def x_faces(self, row, edge):
        upper = self.x_edge(row) if edge == "up" else self.x_face(row)
        lower = self.x_edge(row) if edge == "low" else self.x_face(row - 1)
        return upper, lower

    def edge_of(self, row, boundary):
        return boundary[0] if boundary is not None and boundary[1] == row else None

    def scale(self, row, edge):
        def make():
            upper, lower = self.x_faces(row, edge)
            return 1.0 / ((upper + lower) + self.side_faces(row)[4])

        return self.memo(("h", row, edge), make)

    def weight(self, which, row, edge):
        def make():
            faces = self.x_faces(row, edge) if which < 2 else self.side_faces(row)[:4]
            return faces[which % 2 if which < 2 else which - 2] * self.scale(row, edge)

        return self.stored(("a", which, row, edge), make)

    def drive(self, d, row, edge):
        def make():
            upper, lower = (
                self.x_faces(row, edge) if d == 0 else self.y_faces(row) if d == 1 else self.z_faces(row)
            )
            return (upper - lower) * self.scale(row, edge)

        return self.stored(("c", d, row, edge), make)

    def pressure(self, d, count, row, boundary):
        if boundary is not None and abs(row - boundary[1]) >= count:
            boundary = None
        edge = self.edge_of(row, boundary)
        if count == 1:
            return self.drive(d, row, edge)

        def make():
            a = lambda which: self.weight(which, row, edge)
            here = self.pressure(d, count - 1, row, boundary)
            total = (POLYNOMIAL[SWEEPS - count] / POLYNOMIAL[-1]) * self.drive(d, row, edge)
            side = a(2) * up(here, 1) + a(3) * down(here, 1)
            layers = a(4) * up(here, 0) + a(5) * down(here, 0)
            if edge != "up":
                total = total + a(0) * self.pressure(d, count - 1, row + 1, boundary)
            if edge != "low":
                total = total + a(1) * self.pressure(d, count - 1, row - 1, boundary)
            return total + (side + layers)

        return self.memo(("u", d, count, row, boundary), make)

    def sums(self, d, row, boundary):
        if boundary is not None:
            reach = SWEEPS + (1 if d == 0 and boundary[0] == "up" else 0)
            if abs(row - boundary[1]) >= reach:
                boundary = None

        def make():
            here = self.pressure(d, SWEEPS, row, boundary)
            edge = self.edge_of(row, boundary)
            if d == 0:
                face = self.x_faces(row, edge)[0]
                above = None if edge == "up" else self.pressure(d, SWEEPS, row + 1, boundary)
            elif d == 1:
                face = self.y_faces(row)[0]
                above = up(here, 1)
                if self.y_ends is not None:
                    above = jnp.where(self.y_ends, 0.0, above)
            else:
                face = self.z_faces(row)[0]
                above = jnp.where(self.top, 0.0, up(here, 0))
            drop = 1.0 / POLYNOMIAL[-1] - here
            if above is not None:
                drop = drop + above
            square = drop * drop
            return face * square, square

        return self.memo(("s", d, row, boundary), make)

    def block(self, d, begin, patches):
        uses = {}
        for row in range(begin, begin + BXY):
            for boundary, weight in patches:
                pair = self.sums(d, row, boundary)
                uses.setdefault(id(pair), (pair, []))[1].append(weight)
        groups = {}
        for pair, weights in uses.values():
            groups.setdefault(tuple(map(id, weights)), (weights, []))[1].append(pair)
        totals = None
        for weights, pairs in groups.values():
            part = [functools.reduce(jnp.add, parts) for parts in zip(*pairs)]
            if weights != [None]:
                factor = sum(1.0 if w is None else w for w in weights)
                part = [factor * p for p in part]
            totals = part if totals is None else [a + b for a, b in zip(totals, part)]
        return totals


def accumulate(solver, present):
    low, high, high2 = present
    own = [(("up", BXY - 1), low), (None, None), (("low", 0), high)]
    after = [(("up", 2 * BXY - 1), None), (None, None), (("low", BXY), high2)]
    jobs = [(d, 0, own) for d in range(3)] + [(0, BXY, after)]
    results = {}
    order = [jobs[1], jobs[2], jobs[0], jobs[3]]
    for row in range(BXY):
        for d, begin, patches in order:
            for boundary, _ in patches:
                solver.sums(d, begin + row, boundary)
    for i, (d, begin, patches) in enumerate(jobs):
        results[i] = solver.block(d, begin, patches)
    return [value for i in range(len(jobs)) for value in results[i]]


def thirds(value):
    parts = []
    for _ in range(3):
        parts.append(value.astype(jnp.bfloat16))
        value = value - parts[-1].astype(jnp.float32)
    return parts


def reduce_sums(sums, masks, columns):
    depth = sums[0].shape[0]
    at = lax.broadcasted_iota(jnp.int32, sums[0].shape, 0)
    per = depth // NCL
    rows = []
    for first in range(0, len(sums), per):
        value = None
        for n, total in enumerate(sums[first : first + per]):
            for layer in range(NCL):
                part = total * masks[layer]
                shift = depth // 2
                while shift:
                    part = part + pltpu.roll(part, shift, 0)
                    shift //= 2
                place_at = n * NCL + layer
                value = part if value is None else jnp.where(at < place_at, value, part)
        rows.append(value)
    value = jnp.concatenate(rows, axis=0)
    count = value.shape[0]
    parts = jnp.dot(
        jnp.concatenate(thirds(value), axis=0),
        columns,
        preferred_element_type=jnp.float32,
    )
    return parts[:count] + parts[count : 2 * count] + parts[2 * count :]


def masks_kernel(layer_map, out):
    layer = lax.broadcasted_iota(jnp.int32, out.shape[1:], 0)
    held = jnp.zeros(out.shape[1:], jnp.int32)
    for z in range(out.shape[1]):
        held = jnp.where(layer == z, layer_map[z], held)
    for coarse in range(out.shape[0]):
        out[coarse] = jnp.where(held == coarse, 1.0, 0.0)


def place(axes):
    i, j = (lax.axis_index(a) for a in axes)
    nx, ny = (lax.axis_size(a) for a in axes)
    core, chip = i % 2, i // 2
    one = lambda test: jnp.where(test, 1.0, 0.0).astype(jnp.float32)
    tiles = one(i > 0), one(i < nx - 1), one(i < nx - 2)
    chips = one(chip > 0), one(chip < nx // 2 - 1)
    return core, tiles, chips, (one(j > 0), one(j < ny - 1))


def slots(width):
    return [(comp, row) for row in range(width) for comp in range(3)]


def table_kernel(inside, edges):
    _, _, _, (has_left, has_right) = place(("gx", "gy"))
    lanes = inside.shape[0]
    count, half, start = lanes // BXY, lanes // 2, START
    r = lax.broadcasted_iota(jnp.int32, inside.shape, 0)
    c = lax.broadcasted_iota(jnp.int32, inside.shape, 1)
    inner = (r // BXY == c) & (c > 0) & (c < count - 1)
    inside[...] = jnp.where(inner, 1.0, 0.0).astype(jnp.bfloat16)

    def span(begin):
        return (r >= begin) & (r < begin + BXY)

    first = jnp.where(span(start), 1.0, 0.0) + jnp.where(span(half + start), has_left, 0.0)
    final = jnp.where(span(lanes - BXY), 1.0, 0.0) + jnp.where(span(half - BXY), has_right, 0.0)
    beyond = jnp.where(span(0) | span(half), has_right, 0.0)
    columns = jnp.where(
        c == 0, first, jnp.where(c == count - 1, final, jnp.where(c == count, beyond, 0.0))
    )
    edges[...] = columns.astype(jnp.bfloat16)


def pack_kernel(mine, other, pair, packed):
    core, _, _, _ = place(("gx", "gy"))
    _, depth, width, lanes = mine.shape
    per = lanes // RIGHT
    lane = lanes_of((depth, lanes))
    rows = slots(width)
    count = packed.shape[0] // 2
    for tile, at in ((mine, core), (other, 1 - core)):
        strip = None
        for n, (comp, row) in enumerate(rows):
            value = layers_of(tile, comp, row)
            pair[at * width + row, comp] = value
            shift = RIGHT * (n % per)
            value = pltpu.roll(value, shift + core * START, 1)
            strip = value if n % per == 0 else jnp.where(lane < shift + core * RIGHT, strip, value)
            if n % per == per - 1 or n == len(rows) - 1:
                packed[at * count + n // per] = strip


def join_kernel(below, beside, above, out):
    core, _, (has_down, has_up), (has_left, has_right) = place(("gx", "gy"))
    side = jnp.where(core == 0, has_right, has_left)
    half = beside.shape[0] // 2
    out[:half] = 1.0 / (below[half:] * (side * has_down) + KMIN)
    out[half : 3 * half] = 1.0 / (beside[...] * side + KMIN)
    out[3 * half :] = 1.0 / (above[...] * (side * has_up) + KMIN)


def needed():
    return [(row, comp) for row in range(FIRST, LAST + 1) for comp in range(1 if row in (FIRST, LAST) else 3)]


def with_strips(core, strips, of, width, shape):
    lanes = shape[-1]
    lane = lanes_of(shape)
    begin, end = of * RIGHT, RIGHT + of * LOW
    near = (lane >= begin) & (lane < end)
    far = (lane >= lanes // 2 + begin) & (lane < lanes // 2 + end)
    per, per_tile = lanes // RIGHT, strips.shape[0] // 5
    index = {key: at for at, key in enumerate(slots(width))}

    def put(row, comp, value):
        at = index[comp, row % width]
        strip = strips[(core + 1 + row // width) * per_tile + at // per]
        shift = -RIGHT * (at % per) % lanes
        value = jnp.where(far, pltpu.roll(strip, (shift + lanes // 2) % lanes, 1), value)
        return jnp.where(near, pltpu.roll(strip, shift, 1) if shift else strip, value)

    return put


def putter(stack, placed):
    depth, lanes = stack.shape[2:]
    lane = lanes_of((depth, lanes))
    half, start = lanes // 2, START
    stop = start + BXY + HIGH
    near = (lane >= start) & (lane < stop)
    second = (lane >= half - BXY - LOW) & (lane < half + stop)

    def put(row, comp, value):
        value = 1.0 / (value + KMIN)
        stack[LOW + row, comp] = value
        value = jnp.where(near, pltpu.roll(value, start, 1), value)
        placed[LOW + row, comp] = jnp.where(second, pltpu.roll(value, half, 1), value)

    return put


def within_kernel(pair, stack, placed):
    put = putter(stack, placed)
    for row in range(pair.shape[0]):
        for comp in range(3):
            put(row, comp, pair[row, comp])


def stack_kernel(up_mine, up_other, down_mine, down_other, stack_in, placed_in, stack, placed):
    core, _, (has_down, has_up), _ = place(("gx", "gy"))
    width = up_mine.shape[2]
    first = core == 0
    put = putter(stack, placed)
    for row in range(width):
        for comp in range(3):
            mine, other = layers_of(up_mine, comp, row), layers_of(up_other, comp, row)
            put(2 * width + row, comp, jnp.where(first, mine, other) * has_up)
            if row < HIGH:
                put(3 * width + row, comp, jnp.where(first, other, mine) * has_up)
            if row >= width - LOW:
                mine, other = layers_of(down_mine, comp, row), layers_of(down_other, comp, row)
                put(row - width, comp, jnp.where(first, other, mine) * has_down)


def main_kernel(columns, masks, stack, placed, mine, out, rows, scratch):
    core, present, _, _ = place(("gx", "gy"))
    base = LOW + core * BXY
    solver = Solver(lambda comp, row: stack[base + row, comp], scratch, None, None)
    out[...] = reduce_sums(accumulate(solver, present), masks, columns[...])
    put = with_strips(core, mine, core, BXY, placed.shape[2:])
    for row, comp in needed():
        rows[row - FIRST, comp] = put(row, comp, placed[base + row, comp])


def edge_kernel(columns, masks, rows, other, inner, perm_out, trans_out, scratch):
    core, present, _, _ = place(("gx", "gy"))
    depth, lanes = rows.shape[2:]
    width = BXY
    lane = lanes_of((depth, lanes))
    half, start = lanes // 2, START
    put = with_strips(core, other, 1 - core, width, (depth, lanes))

    def inverse(comp, row):
        return put(row, comp, rows[row - FIRST, comp])

    y_ends = (lane == BXY - 1) | (lane == half + start + BXY - 1)
    y_starts = lane == half - BXY
    solver = Solver(inverse, scratch, y_ends, y_starts)
    sums = accumulate(solver, present)
    count = lanes // BXY
    total = inner[...] + reduce_sums(sums, masks, columns[...])
    cells = (width + 2 * BXY, lanes + 2 * BXY, depth)
    energy = [total[2 * NCL * q : 2 * NCL * q + NCL] for q in range(4)]
    square = [total[2 * NCL * q + NCL : 2 * NCL * (q + 1)] for q in range(4)]
    perms = [
        2.0 * energy[q] / (square[q] + EPS * (cells[d] / POLYNOMIAL[-1]) ** 2)
        for q, d in enumerate((0, 1, 2, 0))
    ]
    layer = lax.broadcasted_iota(jnp.int32, perms[0].shape, 0)
    trans = [
        harmonic(perms[0], perms[3] * present[1]),
        harmonic(perms[1], up(perms[1], 1)),
    ]
    above = jnp.concatenate([perms[2][1:], jnp.zeros_like(perms[2][:1])], axis=0)
    trans.append(harmonic(perms[2], above))
    for d in range(3):
        for l in range(NCL):
            perm_out[d, l, :, :] = perms[d][l : l + 1, :count]
            trans_out[d, l, :, :] = trans[d][l : l + 1, :count]


class Exchange:
    def __init__(self, axes):
        self.axes = axes
        self.nx, self.ny = (lax.axis_size(a) for a in axes)
        self.sent = {}

    def permute(self, value, target):
        nx, ny = self.nx, self.ny
        pairs = []
        for i in range(nx):
            for j in range(ny):
                a, b = target(i, j)
                pairs.append((i * ny + j, a % nx * ny + b))
        key = (id(value), tuple(pairs))
        if key not in self.sent:
            self.sent[key] = (value, lax.ppermute(value, self.axes, pairs))
        return self.sent[key][1]

    def swap(self, value):
        return self.permute(value, lambda i, j: (i ^ 1, j))

    def straight(self, value, pairs):
        return self.permute(value, lambda i, j: (i - 2 * pairs, j))

    def sideways(self, value, pairs):
        def target(i, j):
            to = j - 1 if i % 2 == 0 else j + 1
            i -= 2 * pairs
            return (i, to) if 0 <= to < self.ny else (i ^ 1, j)

        return self.permute(value, target)


def local(permeability, layer_map):
    _, depth, width, lanes = permeability.shape
    net = Exchange(("gx", "gy"))
    if width != BXY or depth != 8 or lanes != 128 or net.nx % 2:
        raise ValueError("unsupported tile")
    vmem = pl.BlockSpec(memory_space=pltpu.VMEM)
    smem = pl.BlockSpec(memory_space=pltpu.SMEM)
    limit = pltpu.CompilerParams(vmem_limit_bytes=16 << 20)
    held = lambda value: pltpu.with_memory_space_constraint(value, pltpu.VMEM)
    strips = -(-len(slots(width)) // (lanes // RIGHT))

    inside, edges = pl.pallas_call(
        table_kernel,
        out_shape=[pltpu.VMEM((lanes, lanes), jnp.bfloat16)] * 2,
        out_specs=[vmem] * 2,
        compiler_params=limit,
        cost_estimate=pl.CostEstimate(flops=LONG, bytes_accessed=lanes * lanes * 4, transcendentals=0),
    )()
    other = net.swap(permeability)
    up, down = net.straight(permeability, 1), net.straight(permeability, -1)
    pair, packed = pl.pallas_call(
        pack_kernel,
        out_shape=[
            pltpu.VMEM((2 * width, 3, depth, lanes), jnp.float32),
            pltpu.VMEM((2 * strips, depth, lanes), jnp.float32),
        ],
        in_specs=[vmem] * 2,
        out_specs=[vmem] * 2,
        compiler_params=limit,
    )(held(permeability), held(other))
    above, below = net.sideways(packed, 1), net.sideways(packed, -1)
    beside = net.sideways(packed, 0)
    up_other, down_other = net.swap(up), net.swap(down)
    masks = pl.pallas_call(
        masks_kernel,
        out_shape=pltpu.VMEM((NCL, depth, lanes), jnp.float32),
        in_specs=[smem],
        out_specs=vmem,
        compiler_params=limit,
    )(layer_map)
    scratch = pltpu.VMEM((256, depth, lanes), jnp.float32)
    rows = LOW + 3 * width + HIGH
    shapes = [pltpu.VMEM((rows, 3, depth, lanes), jnp.float32)] * 2
    stack, placed = pl.pallas_call(
        within_kernel,
        out_shape=shapes,
        in_specs=[vmem],
        out_specs=[vmem] * 2,
        compiler_params=limit,
    )(held(pair))
    stack, placed = pl.pallas_call(
        stack_kernel,
        out_shape=shapes,
        in_specs=[vmem] * 6,
        out_specs=[vmem] * 2,
        input_output_aliases={4: 0, 5: 1},
        compiler_params=limit,
        cost_estimate=pl.CostEstimate(flops=LONG, bytes_accessed=4 * permeability.size * 4, transcendentals=0),
    )(held(up), held(up_other), held(down), held(down_other), held(stack), held(placed))
    joined = pl.pallas_call(
        join_kernel,
        out_shape=pltpu.VMEM((5 * strips, depth, lanes), jnp.float32),
        in_specs=[vmem] * 3,
        out_specs=vmem,
        compiler_params=limit,
    )(held(below), held(beside), held(above))
    theirs = net.swap(joined)
    inner, near = pl.pallas_call(
        main_kernel,
        out_shape=[
            pltpu.VMEM((8 * NCL, lanes), jnp.float32),
            pltpu.VMEM((LAST + 1 - FIRST, 3, depth, lanes), jnp.float32),
        ],
        in_specs=[vmem] * 5,
        out_specs=[vmem] * 2,
        scratch_shapes=[scratch],
        compiler_params=limit,
        cost_estimate=pl.CostEstimate(flops=LONG, bytes_accessed=4 * permeability.size * 4, transcendentals=0),
    )(held(inside), held(masks), held(stack), held(placed), held(joined))
    out = jax.ShapeDtypeStruct((3, NCL, width // BXY, lanes // BXY), jnp.float32)
    return pl.pallas_call(
        edge_kernel,
        out_shape=(out, out),
        in_specs=[vmem] * 5,
        out_specs=(vmem, vmem),
        scratch_shapes=[scratch],
        compiler_params=limit,
    )(held(edges), held(masks), held(near), held(theirs), held(inner))


def solution(mesh):
    in_specs = (P(None, None, "gx", "gy"), P())
    out_specs = (P(None, None, "gx", "gy"), P(None, None, "gx", "gy"))
    return jax.shard_map(local, mesh=mesh, in_specs=in_specs, out_specs=out_specs, check_vma=False)
```
